256 devices in a mesh: layer: 128 (over z, y, x), batch: 2 (over core).
Axes of the slice: x: 4, y: 4, z: 8, core: 2. Of those that a mesh axis runs over, the one named last changes fastest.
Arguments:
- kernels: bfloat16 [512, 9, 128, 128], P('layer'), may hold values from -0.1875 to 0.1875
- biases: float32 [512, 128], P('layer'), may hold values from -3 to 3
- states: float32 [128, 2, 16, 16, 128], P('layer', 'batch'), may hold values from -6 to 6
- adjoint_guess: float32 [128, 2, 16, 16, 128], P('layer', 'batch'), may hold values from -6 to 6
Outputs:
- new_states: float32 [128, 2, 16, 16, 128], P('layer', 'batch')
- new_ends: float32 [128, 2, 16, 16, 128], P('layer', 'batch')
- new_adjoint: float32 [128, 2, 16, 16, 128], P('layer', 'batch')
- new_back_starts: float32 [128, 2, 16, 16, 128], P('layer', 'batch')
- grad_kernel: float32 [512, 9, 128, 128], P('layer')
- grad_bias: float32 [512, 128], P('layer')
The draws below stay inside these ranges and needn't reach their ends.
All inputs are finite; a program needn't handle non-finite values.
Results may differ from the reference program's by a relative error of at most 0.0094.
Values sent between devices are 32-bit elements; how exact they have to be, the bound alone decides.
A program may use at most 128 MiB of HBM per device.

```python
import jax
import jax.numpy as jnp
from jax import lax

CH = 128
SIDE = 16
BLOCKS = 4
LAYERS = 512
BATCH = 2
N_LAYER = 128


def shard_levels(key, shape, cuts, smallest, high):
    factor_of = 1.0
    for dim, parts in cuts:
        heights = jax.random.uniform(jax.random.fold_in(jax.random.fold_in(key, 6), dim), (parts,), jnp.float32, smallest / len(cuts), high / len(cuts))
        factor_of = factor_of * jnp.repeat(jnp.exp(heights), shape[dim] // parts).reshape((-1,) + (1,) * (len(shape) - 1 - dim))
    return factor_of


def bell_draw(own_key, dims, width, most, cuts=(), held_as=jnp.bfloat16):
    array = width * jax.random.normal(own_key, dims, jnp.float32)
    if cuts:
        array = array * shard_levels(own_key, dims, cuts, -0.22, 0.18)
    return jnp.clip(array, -most, most).astype(held_as)


def setup_inputs(seed: int = 0) -> dict:
    key_of = jax.random.split(jax.random.key(seed), 5)
    kernels = bell_draw(key_of[0], (LAYERS, 9, CH, CH), (9 * CH) ** -0.5, 0.1875, ((0, 128),))
    biases = bell_draw(key_of[1], (LAYERS, CH), 0.5, 3.0, ((0, 128),), jnp.float32)
    states = bell_draw(key_of[2], (N_LAYER, BATCH, SIDE, SIDE, CH), 1.0, 6.0, ((0, 128), (1, 2)), jnp.float32)
    adjoint_guess = bell_draw(key_of[3], (N_LAYER, BATCH, SIDE, SIDE, CH), 1.0, 6.0, ((0, 128), (1, 2)), jnp.float32)
    return dict(kernels=kernels, biases=biases, states=states, adjoint_guess=adjoint_guess)


STEP_SIZE = 0.1


def patches(image):
    extent = image.shape[1]
    padded = jnp.pad(image, ((0, 0), (1, 1), (1, 1), (0, 0)))
    shifted = [padded[:, row_shift:row_shift + extent, col_shift:col_shift + extent, :] for row_shift in range(3) for col_shift in range(3)]
    return jnp.concatenate(shifted, axis=-1)


def convolve(image, weights_flat):
    return jnp.dot(patches(image), weights_flat, preferred_element_type=jnp.float32)


def forward_step(state, weights_flat, bias_row):
    pre_act = convolve(state.astype(jnp.bfloat16), weights_flat) + bias_row
    return state + STEP_SIZE * jnp.tanh(pre_act)


def adjoint_step(adjoint, slope, flipped):
    sens = (slope * adjoint).astype(jnp.bfloat16)
    return adjoint + STEP_SIZE * convolve(sens, flipped)


def full_dot(left, right):
    return jnp.dot(left, right, precision=lax.Precision.HIGHEST, preferred_element_type=jnp.float32)


def reference(kernels, biases, states, adjoint_guess):
    kernel_set = kernels.reshape(N_LAYER, BLOCKS, 9, CH, CH)
    weights_all = kernel_set.reshape(N_LAYER, BLOCKS, 9 * CH, CH)
    flipped_all = jnp.transpose(kernel_set[:, :, ::-1], (0, 1, 2, 4, 3)).reshape(N_LAYER, BLOCKS, 9 * CH, CH)
    bias_all = biases.reshape(N_LAYER, BLOCKS, CH)
    unit = jnp.eye(CH, dtype=jnp.float32)
    centre = kernel_set[:, 0, 4].astype(jnp.float32)
    interval_ids = jnp.arange(N_LAYER, dtype=jnp.int32)[:, None, None]

    def relax_once(inputs):
        weights_here, bias_here, state = inputs
        for offset in range(BLOCKS - 1):
            state = forward_step(state, weights_here[offset], bias_here[offset])
        return forward_step(state, weights_here[BLOCKS - 1], bias_here[BLOCKS - 1])

    def times_map(inputs):
        field, matrix = inputs
        return full_dot(field, matrix)

    relaxed = lax.map(relax_once, (weights_all, bias_all, states))
    start = jnp.concatenate([states[:1], relaxed[:-1]], axis=0)
    coarse = jnp.where(interval_ids == 0, jnp.zeros_like(centre), unit + BLOCKS * STEP_SIZE * centre)
    carry_term = lax.map(relax_once, (weights_all, bias_all, start)) - lax.map(times_map, (start, coarse))

    def advance(carried, inputs):
        matrix, term = inputs
        return full_dot(carried, matrix) + term, carried

    _, new_states = lax.scan(advance, states[0], (coarse, carry_term))
    new_ends = lax.map(times_map, (new_states, coarse)) + carry_term

    def final_forward(inputs):
        weights_here, bias_here, state = inputs
        inputs_list = []
        slopes = []
        for offset in range(BLOCKS):
            rounded = state.astype(jnp.bfloat16)
            activ = jnp.tanh(convolve(rounded, weights_here[offset]) + bias_here[offset])
            inputs_list.append(rounded)
            slopes.append(1.0 - activ * activ)
            state = state + STEP_SIZE * activ
        return jnp.stack(inputs_list), jnp.stack(slopes)

    block_inputs, slopes_all = lax.map(final_forward, (weights_all, bias_all, new_states))

    def back_relax(inputs):
        flipped_here, slope_here, adjoint = inputs
        for offset in range(BLOCKS - 1, 0, -1):
            adjoint = adjoint_step(adjoint, slope_here[offset], flipped_here[offset])
        return adjoint_step(adjoint, slope_here[0], flipped_here[0])

    back_relaxed = lax.map(back_relax, (flipped_all, slopes_all, adjoint_guess))
    back_start = jnp.concatenate([back_relaxed[1:], adjoint_guess[-1:]], axis=0)
    back_coarse = jnp.where(interval_ids == N_LAYER - 1, jnp.zeros_like(centre), unit + BLOCKS * STEP_SIZE * jnp.transpose(centre, (0, 2, 1)))
    back_carry_term = lax.map(back_relax, (flipped_all, slopes_all, back_start)) - lax.map(times_map, (back_start, back_coarse))
    _, new_adjoint = lax.scan(advance, adjoint_guess[-1], (back_coarse, back_carry_term), reverse=True)
    new_back_starts = lax.map(times_map, (new_adjoint, back_coarse)) + back_carry_term
    factor = STEP_SIZE / (BATCH * SIDE * SIDE)

    def gradients(inputs):
        flipped_here, slope_here, input_here, adjoint = inputs
        kernel_terms = [None] * BLOCKS
        bias_terms = [None] * BLOCKS
        for offset in range(BLOCKS - 1, -1, -1):
            sens = (slope_here[offset] * adjoint).astype(jnp.bfloat16)
            columns = patches(input_here[offset]).astype(jnp.float32)
            kernel_terms[offset] = jnp.einsum("bhwk,bhwc->kc", columns, sens.astype(jnp.float32))
            bias_terms[offset] = jnp.sum(sens.astype(jnp.float32), axis=(0, 1, 2))
            if offset > 0:
                adjoint = adjoint + STEP_SIZE * convolve(sens, flipped_here[offset])
        return jnp.stack(kernel_terms), jnp.stack(bias_terms)

    kernel_grads, bias_grads = lax.map(gradients, (flipped_all, slopes_all, block_inputs, new_adjoint))
    grad_kernel = (factor * kernel_grads).reshape(LAYERS, 9, CH, CH)
    grad_bias = (factor * bias_grads).reshape(LAYERS, CH)
    return new_states, new_ends, new_adjoint, new_back_starts, grad_kernel, grad_bias
```

```python
import functools

import jax
import jax.numpy as jnp
from jax import lax
from jax.experimental import pallas as pl
from jax.experimental.pallas import tpu as pltpu
from jax.sharding import Mesh
from jax.sharding import PartitionSpec as P

LAYER = ("layer_0", "layer_1", "layer_2")
AXES = LAYER + ("batch",)
MESH = pl.DeviceIdType.MESH
STEP = 0.1
F32 = jnp.float32
BF16 = jnp.bfloat16


def split(value):
    high = value.astype(BF16)
    return high, (value - high.astype(F32)).astype(BF16)


def dot(left, right, flip=False):
    contract = (((1,), (1,)), ((), ())) if flip else (((1,), (0,)), ((), ()))
    return lax.dot_general(left, right, contract, preferred_element_type=F32)


def times_exact(left, exact, flip=False):
    high, low = split(left)
    return dot(high, exact, flip) + dot(low, exact, flip)


def exact_times(exact, right):
    high, low = split(right)
    return dot(exact, high) + dot(exact, low)


def times(left, right, flip=False):
    high, low = split(left)
    right_high, right_low = split(right)
    return dot(high, right_high, flip) + (dot(low, right_high, flip) + dot(high, right_low, flip))


def kernel(
    sizes, blocks, side, batch,
    k_hbm, b_hbm, st_hbm, ad_hbm,
    ns_out, ne_out, na_out, nb_out, gk_out, gb_out,
    w, bias, states, guess,
    xs, xt, slopes,
    kx, ry, pz, pm, sm, pr, sr,
    shift_src, shift_dst, c_buf, v_src, v_dst,
    w_src, up, tz, row_src, down, results, lam_ref,
    g_own, g_got, gb_own, gb_got,
    in_sem, out_sem,
    mat_s, mat_r, pair_s, pair_r,
    shift_s, shift_r, chain_s, chain_r,
    up_s, up_r, z_s, z_r, down_s, down_r,
    g_s, g_r, gb_s, gb_r,
):
    nz, ny, nx, nb = sizes
    plane = ny * nx
    ch = w.shape[-1]
    cells = side * side
    own_cells = cells // plane
    coarse_step = blocks * STEP
    z, y, x = (lax.axis_index(a) for a in LAYER)
    b = lax.axis_index("batch")
    me = y * nx + x
    pos = z * plane + me
    last = nz * plane - 1
    first = pos == 0
    final = pos == last

    def device(position):
        return (position // plane, lax.rem(position // nx, ny), lax.rem(position, nx), b)

    ahead = device(lax.rem(pos + 1, last + 1))
    behind = device(lax.rem(pos + last, last + 1))
    partner = (z, y, x, 1 - b)

    def mate(k):
        t = lax.rem(me + k, plane)
        return t, (z, t // nx, lax.rem(t, nx), b)

    def copy(src, dst, send, recv, to):
        return pltpu.make_async_remote_copy(
            src_ref=src, dst_ref=dst, send_sem=send, recv_sem=recv, device_id=to, device_id_type=MESH
        )

    loads = [
        pltpu.make_async_copy(st_hbm, states, in_sem.at[0]),
        pltpu.make_async_copy(b_hbm, bias, in_sem.at[1]),
        pltpu.make_async_copy(ad_hbm, guess, in_sem.at[2]),
    ] + [pltpu.make_async_copy(k_hbm.at[n], w.at[n], in_sem.at[3 + n]) for n in range(blocks)]
    for c in loads:
        c.start()

    barrier = pltpu.get_barrier_semaphore()

    def greet(to):
        pl.semaphore_signal(barrier, inc=1, device_id=to, device_id_type=MESH)

    greet(ahead)
    greet(behind)
    greet(partner)
    for k in range(1, plane):
        greet(mate(k)[1])
    for k in range(1, nz):
        greet((lax.rem(z + k, nz), y, x, b))
    greeted = 3 + plane - 1 + nz - 1

    for d in range(3):
        xs[d, 0:side, :] = jnp.zeros((side, ch), BF16)
        xs[d, side + cells : 2 * side + cells, :] = jnp.zeros((side, ch), BF16)
    column = lax.rem(lax.broadcasted_iota(jnp.int32, (cells, ch), 0), side)
    inner_left = column != 0
    inner_right = column != side - 1
    for c in loads:
        c.wait()

    def place(value):
        xs[1, side : side + cells, :] = value.astype(BF16)
        xs[0, side : side + cells, :] = jnp.where(inner_left, pltpu.roll(value, 1, 0), 0.0).astype(BF16)
        xs[2, side : side + cells, :] = jnp.where(inner_right, pltpu.roll(value, cells - 1, 0), 0.0).astype(BF16)

    def patches():
        return jnp.concatenate(
            [xs[dx, side * dy : side * dy + cells, :] for dy in range(3) for dx in range(3)], axis=1
        )

    def activate(n, u):
        place(u)
        return jnp.tanh(dot(patches(), w[n]) + bias[pl.ds(n, 1), :])

    def adjoint_conv(n, columns):
        flipped = jnp.concatenate([w[n, ch * (8 - t) : ch * (9 - t), :] for t in range(9)], axis=1)
        return dot(columns, flipped, True)

    def relax(u):
        return lax.fori_loop(0, blocks, lambda n, s: s + STEP * activate(n, s), u)

    def back_relax(lam):
        def body(k, lam):
            n = blocks - 1 - k
            place(slopes[n] * lam)
            return lam + STEP * adjoint_conv(n, patches())

        return lax.fori_loop(0, blocks, body, lam)

    eye = (
        lax.broadcasted_iota(jnp.int32, (ch, ch), 0) == lax.broadcasted_iota(jnp.int32, (ch, ch), 1)
    ).astype(F32)
    centre = w[0, 4 * ch : 5 * ch, :]
    half = ch // nb
    mine = pl.ds(pl.multiple_of(half * b, half), half)
    other = pl.ds(pl.multiple_of(half * (1 - b), half), half)

    def mats(level, buf, index, size, to):
        def start():
            for k in range(1, size):
                copy(
                    buf.at[index, mine], buf.at[index, mine], mat_s.at[level, k], mat_r.at[level, k],
                    to(lax.rem(index + k, size)),
                ).start()

        def relay():
            for k in range(1, size):
                source = lax.rem(index - k + size, size)
                copy(
                    buf.at[source, mine], buf.at[source, mine], mat_s.at[level, k], mat_r.at[level, k], partner
                ).wait_recv()
                copy(
                    buf.at[source, mine], buf.at[source, mine], pair_s.at[level, k], pair_r.at[level, k], partner
                ).start()

        def finish():
            for k in range(1, size):
                source = lax.rem(index - k + size, size)
                copy(
                    buf.at[source, other], buf.at[source, other], pair_s.at[level, k], pair_r.at[level, k], partner
                ).wait_recv()

        def drain():
            for k in range(1, size):
                source = lax.rem(index - k + size, size)
                copy(
                    buf.at[index, mine], buf.at[index, mine], mat_s.at[level, k], mat_r.at[level, k], partner
                ).wait_send()
                copy(
                    buf.at[source, mine], buf.at[source, mine], pair_s.at[level, k], pair_r.at[level, k], partner
                ).wait_send()

        return start, relay, finish, drain

    row_mats = mats(0, kx, x, nx, lambda t: (z, y, t, b))
    column_mats = mats(1, ry, y, ny, lambda t: (z, t, x, b))
    z_mats = mats(2, pz, z, nz, lambda t: (t, y, x, b))

    kx[x] = centre.astype(F32)
    relaxed = relax(states[...])
    pl.semaphore_wait(barrier, greeted)
    row_mats[0]()
    shift_src[0] = relaxed
    forward_shift = copy(shift_src.at[0], shift_dst.at[0], shift_s.at[0], shift_r.at[0], ahead)
    forward_shift.start()

    row_mats[1]()
    row_mats[2]()
    pm[0] = eye
    for j in range(nx):
        pm[j + 1] = pm[j] + coarse_step * times_exact(pm[j], kx[j].astype(BF16))
    sm[nx - 1] = eye
    for j in range(nx - 1, 0, -1):
        sm[j - 1] = sm[j] + coarse_step * exact_times(kx[j].astype(BF16), sm[j])
    ry[y] = pm[nx]
    column_mats[0]()

    def coarse_of(field, flip):
        return field + coarse_step * times_exact(field, centre, flip)

    def scan(d, extra_up, extra_z):
        flip = d == 1
        row_later, row_sooner = (pm, sm) if flip else (sm, pm)
        column_later, column_sooner = (pr, sr) if flip else (sr, pr)
        w_src[d] = times(c_buf[d], row_later[x], flip)
        for k in range(1, plane):
            t, to = mate(k)
            piece = pl.ds(pl.multiple_of(own_cells * t, own_cells), own_cells)
            copy(w_src.at[d, piece], up.at[d, me], up_s.at[d, k], up_r.at[d, k], to).start()
        own = pl.ds(pl.multiple_of(own_cells * me, own_cells), own_cells)
        up[d, me] = w_src[d, own]

        def chain_copy():
            to = lax.rem(x + (nx - 1 if flip else 1), nx)
            return copy(v_src.at[d], v_dst.at[d], chain_s.at[d], chain_r.at[d], (z, y, to, b))

        def chain(k):
            sender = nx - 1 - k if flip else k
            if k >= nx - 1:
                return

            @pl.when(x == sender)
            def _():
                if k == 0:
                    v_src[d] = c_buf[d]
                else:
                    chain_copy().wait_recv()
                    v_src[d] = coarse_of(v_dst[d], flip) + c_buf[d]
                chain_copy().start()

        chain(0)
        extra_up()
        for k in range(1, plane):
            source = lax.rem(me - k + plane, plane)
            copy(w_src.at[d, own], up.at[d, source], up_s.at[d, k], up_r.at[d, k], partner).wait_recv()
        row_total = [sum(up[d, r * nx + i] for i in range(nx)) for r in range(ny)]
        tz[d, z] = sum(times(row_total[r], column_later[r], flip) for r in range(ny))
        for k in range(1, nz):
            to = lax.rem(z + k, nz)
            copy(tz.at[d, z], tz.at[d, z], z_s.at[d, k], z_r.at[d, k], (to, y, x, b)).start()
        inside = [None] * ny
        order = list(range(ny - 1, -1, -1)) if flip else list(range(ny))
        inside[order[0]] = jnp.zeros((own_cells, ch), F32)
        for r, s in zip(order, order[1:]):
            inside[s] = times(inside[r], ry[r], flip) + row_total[r]
        chain(1)
        extra_z()
        for k in range(1, nz):
            source = lax.rem(z - k + nz, nz)
            copy(tz.at[d, source], tz.at[d, source], z_s.at[d, k], z_r.at[d, k], partner).wait_recv()

        def advance(k, s):
            i = nz - 1 - k if flip else k
            return times(s, pz[i], flip) + tz[d, i]

        entering = lax.fori_loop(0, nz - 1 - z if flip else z, advance, jnp.zeros((own_cells, ch), F32))
        for r in range(ny):
            row_src[d, r] = times(entering, column_sooner[r], flip) + inside[r]
        for k in range(1, plane):
            t, to = mate(k)
            copy(row_src.at[d, t // nx], down.at[d, own], down_s.at[d, k], down_r.at[d, k], to).start()
        down[d, own] = row_src[d, y]
        for k in range(2, nx - 1):
            chain(k)
        for k in range(1, plane):
            source = lax.rem(me - k + plane, plane)
            piece = pl.ds(pl.multiple_of(own_cells * source, own_cells), own_cells)
            copy(row_src.at[d, y], down.at[d, piece], down_s.at[d, k], down_r.at[d, k], partner).wait_recv()
        results[d] = times(down[d], row_sooner[x], flip)

        @pl.when(x == (0 if flip else nx - 1))
        def _():
            chain_copy().wait_recv()

        @pl.when(x != (nx - 1 if flip else 0))
        def _():
            results[d] = results[d] + v_dst[d]

        def drain():
            for k in range(1, plane):
                copy(w_src.at[d, own], up.at[d, me], up_s.at[d, k], up_r.at[d, k], partner).wait_send()
                copy(row_src.at[d, y], down.at[d, own], down_s.at[d, k], down_r.at[d, k], partner).wait_send()
            for k in range(1, nz):
                copy(tz.at[d, z], tz.at[d, z], z_s.at[d, k], z_r.at[d, k], partner).wait_send()

            @pl.when(x != (0 if flip else nx - 1))
            def _():
                chain_copy().wait_send()

        return drain

    forward_shift.wait_recv()
    start = jnp.where(first, states[...], shift_dst[0])
    c_buf[0] = jnp.where(first, 0.0, -coarse_of(start, False)) + relax(start)

    def extra_up():
        column_mats[1]()
        column_mats[2]()
        pr[0] = eye
        for j in range(ny):
            pr[j + 1] = times(pr[j], ry[j])
        sr[ny - 1] = eye
        for j in range(ny - 1, 0, -1):
            sr[j - 1] = times(ry[j], sr[j])
        pz[z] = pr[ny]
        z_mats[0]()

    def extra_z():
        z_mats[1]()
        z_mats[2]()

    forward_drain = scan(0, extra_up, extra_z)
    results[0] = jnp.where(first, states[...], results[0])
    outs = [pltpu.make_async_copy(results.at[0], ns_out, out_sem.at[0])]
    outs[0].start()

    def final_step(n, u):
        activ = activate(n, u)
        xt[n] = jnp.transpose(xs[1, side : side + cells, :].astype(F32)).astype(BF16)
        slopes[n] = 1.0 - activ * activ
        return u + STEP * activ

    lax.fori_loop(0, blocks, final_step, results[0])

    shift_src[1] = back_relax(guess[...])
    back_shift = copy(shift_src.at[1], shift_dst.at[1], shift_s.at[1], shift_r.at[1], behind)
    back_shift.start()
    new_ends = jnp.where(first, 0.0, coarse_of(results[0], False)) + c_buf[0]
    v_src[2] = new_ends
    outs.append(pltpu.make_async_copy(v_src.at[2], ne_out, out_sem.at[1]))
    outs[-1].start()
    back_shift.wait_recv()
    back_start = jnp.where(final, guess[...], shift_dst[1])
    c_buf[1] = jnp.where(final, 0.0, -coarse_of(back_start, True)) + back_relax(back_start)
    back_drain = scan(1, lambda: None, lambda: None)
    results[1] = jnp.where(final, guess[...], results[1])
    outs.append(pltpu.make_async_copy(results.at[1], na_out, out_sem.at[2]))
    outs[-1].start()

    def grad_copy(n):
        return copy(g_own.at[n], g_got.at[n], g_s.at[n], g_r.at[n], partner)

    lam_ref[...] = results[1]
    for n in range(blocks - 1, -1, -1):
        sens = slopes[n] * lam_ref[...]
        place(sens)
        columns = patches()
        if n > 0:
            lam_ref[...] = lam_ref[...] + STEP * adjoint_conv(n, columns)
        gb_own[n : n + 1, :] = jnp.sum(sens.astype(BF16).astype(F32), axis=0, keepdims=True)
        product = dot(xt[n], columns)
        for t in range(9):
            g_own[n, t] = product[:, ch * (8 - t) : ch * (9 - t)]
        grad_copy(n).start()
    bias_copy = copy(gb_own, gb_got, gb_s, gb_r, partner)
    bias_copy.start()
    new_back = jnp.where(final, 0.0, coarse_of(results[1], True)) + c_buf[1]
    v_src[3] = new_back
    outs.append(pltpu.make_async_copy(v_src.at[3], nb_out, out_sem.at[3]))
    outs[-1].start()
    factor = STEP / (nb * batch * cells)
    for n in range(blocks - 1, -1, -1):
        grad_copy(n).wait_recv()
        g_got[n] = factor * (g_own[n] + g_got[n])
        outs.append(pltpu.make_async_copy(g_got.at[n], gk_out.at[n], out_sem.at[4 + n]))
        outs[-1].start()
    bias_copy.wait_recv()
    gb_got[...] = factor * (gb_own[...] + gb_got[...])
    outs.append(pltpu.make_async_copy(gb_got, gb_out, out_sem.at[4 + blocks]))
    outs[-1].start()

    for n in range(blocks):
        grad_copy(n).wait_send()
    bias_copy.wait_send()
    forward_shift.wait_send()
    back_shift.wait_send()
    row_mats[3]()
    column_mats[3]()
    z_mats[3]()
    forward_drain()
    back_drain()
    for c in outs:
        c.wait()


def body(sizes, kernels, biases, states, adjoint_guess):
    nz, ny, nx, nb = sizes
    plane = ny * nx
    blocks, taps, ch, _ = kernels.shape
    side = states.shape[2]
    batch = states.shape[1]
    cells = side * side
    own = cells // plane
    field = jax.ShapeDtypeStruct((cells, ch), F32)
    dma = pltpu.SemaphoreType.DMA
    most = max(nz, ny, nx)
    vmem = pltpu.VMEM
    scratch = [
        vmem((blocks, taps * ch, ch), BF16),
        vmem((blocks, ch), F32),
        vmem((cells, ch), F32),
        vmem((cells, ch), F32),
        vmem((3, cells + 2 * side, ch), BF16),
        vmem((blocks, ch, cells), BF16),
        vmem((blocks, cells, ch), F32),
        vmem((nx, ch, ch), F32),
        vmem((ny, ch, ch), F32),
        vmem((nz, ch, ch), F32),
        vmem((nx + 1, ch, ch), F32),
        vmem((nx, ch, ch), F32),
        vmem((ny + 1, ch, ch), F32),
        vmem((ny, ch, ch), F32),
        vmem((2, cells, ch), F32),
        vmem((2, cells, ch), F32),
        vmem((2, cells, ch), F32),
        vmem((4, cells, ch), F32),
        vmem((2, cells, ch), F32),
        vmem((2, cells, ch), F32),
        vmem((2, plane, own, ch), F32),
        vmem((2, nz, own, ch), F32),
        vmem((2, ny, own, ch), F32),
        vmem((2, cells, ch), F32),
        vmem((2, cells, ch), F32),
        vmem((cells, ch), F32),
        vmem((blocks, taps, ch, ch), F32),
        vmem((blocks, taps, ch, ch), F32),
        vmem((blocks, ch), F32),
        vmem((blocks, ch), F32),
        dma((3 + blocks,)),
        dma((5 + blocks,)),
        dma((3, most)),
        dma((3, most)),
        dma((3, most)),
        dma((3, most)),
        dma((2,)),
        dma((2,)),
        dma((2,)),
        dma((2,)),
        dma((2, plane)),
        dma((2, plane)),
        dma((2, nz)),
        dma((2, nz)),
        dma((2, plane)),
        dma((2, plane)),
        dma((blocks,)),
        dma((blocks,)),
        dma(()),
        dma(()),
    ]
    any_space = pl.BlockSpec(memory_space=pl.ANY)
    outs = pl.pallas_call(
        functools.partial(kernel, sizes, blocks, side, batch),
        out_shape=[field] * 4
        + [jax.ShapeDtypeStruct((blocks, taps, ch, ch), F32), jax.ShapeDtypeStruct((blocks, ch), F32)],
        in_specs=[any_space] * 4,
        out_specs=[any_space] * 6,
        scratch_shapes=scratch,
        compiler_params=pltpu.CompilerParams(
            collective_id=0, has_side_effects=True, vmem_limit_bytes=40 * 1024 * 1024
        ),
        name="vcycle",
    )(
        kernels.reshape(blocks, taps * ch, ch),
        biases,
        states.reshape(cells, ch),
        adjoint_guess.reshape(cells, ch),
    )
    fields = [out.reshape(states.shape) for out in outs[:4]]
    return (*fields, outs[4], outs[5])


def solution(mesh, sizes=(8, 4, 4)):
    sizes = (*sizes, mesh.shape["batch"])
    torus = Mesh(mesh.devices.reshape(sizes), AXES)
    state = P(LAYER, "batch", None, None, None)
    return jax.shard_map(
        functools.partial(body, sizes),
        mesh=torus,
        in_specs=(P(LAYER, None, None, None), P(LAYER, None), state, state),
        out_specs=(state, state, state, state, P(LAYER, None, None, None), P(LAYER, None)),
        check_vma=False,
    )
```

```python
import functools

import jax
import jax.numpy as jnp
from jax import lax
from jax.experimental import pallas as pl
from jax.experimental.pallas import tpu as pltpu
from jax.sharding import Mesh
from jax.sharding import PartitionSpec as P

LAYER = ("layer_0", "layer_1", "layer_2")
AXES = LAYER + ("batch",)
MESH = pl.DeviceIdType.MESH
STEP = 0.1
F32 = jnp.float32
BF16 = jnp.bfloat16


def split(value):
    high = value.astype(BF16)
    return high, (value - high.astype(F32)).astype(BF16)


def dot(left, right, flip=False):
    contract = (((1,), (1,)), ((), ())) if flip else (((1,), (0,)), ((), ()))
    return lax.dot_general(left, right, contract, preferred_element_type=F32)


def times_exact(left, exact, flip=False):
    high, low = split(left)
    return dot(high, exact, flip) + dot(low, exact, flip)


def exact_times(exact, right):
    high, low = split(right)
    return dot(exact, high) + dot(exact, low)


def times(left, right, flip=False):
    high, low = split(left)
    right_high, right_low = split(right)
    return dot(high, right_high, flip) + (dot(low, right_high, flip) + dot(high, right_low, flip))


def kernel(
    sizes, blocks, side, batch,
    k_hbm, b_hbm, st_hbm, ad_hbm,
    ns_out, ne_out, na_out, nb_out, gk_out, gb_out,
    w, bias, states, guess,
    xs, xt, slopes,
    kx, ry, pz, pm, sm, pr, sr,
    shift_src, shift_dst, c_buf, v_src, v_dst,
    w_src, up, tz, row_src, down, results, lam_ref,
    u_own, u_got, xt_got, sens_own, sens_got, g_own, g_sum, gb_sum,
    in_sem, out_sem,
    mat_s, mat_r, pair_s, pair_r,
    shift_s, shift_r, chain_s, chain_r,
    up_s, up_r, z_s, z_r, down_s, down_r,
    u_s, u_r, sens_s, sens_r,
):
    nz, ny, nx, nb = sizes
    plane = ny * nx
    ch = w.shape[-1]
    cells = side * side
    own_cells = cells // plane
    coarse_step = blocks * STEP
    z, y, x = (lax.axis_index(a) for a in LAYER)
    b = lax.axis_index("batch")
    me = y * nx + x
    pos = z * plane + me
    last = nz * plane - 1
    first = pos == 0
    final = pos == last

    def device(position):
        return (position // plane, lax.rem(position // nx, ny), lax.rem(position, nx), b)

    ahead = device(lax.rem(pos + 1, last + 1))
    behind = device(lax.rem(pos + last, last + 1))
    partner = (z, y, x, 1 - b)

    def mate(k):
        t = lax.rem(me + k, plane)
        return t, (z, t // nx, lax.rem(t, nx), b)

    def copy(src, dst, send, recv, to):
        return pltpu.make_async_remote_copy(
            src_ref=src, dst_ref=dst, send_sem=send, recv_sem=recv, device_id=to, device_id_type=MESH
        )

    loads = [
        pltpu.make_async_copy(st_hbm, states, in_sem.at[0]),
        pltpu.make_async_copy(b_hbm, bias, in_sem.at[1]),
        pltpu.make_async_copy(ad_hbm, guess, in_sem.at[2]),
    ] + [pltpu.make_async_copy(k_hbm.at[n], w.at[n], in_sem.at[3 + n]) for n in range(blocks)]
    for c in loads:
        c.start()

    barrier = pltpu.get_barrier_semaphore()

    def greet(to):
        pl.semaphore_signal(barrier, inc=1, device_id=to, device_id_type=MESH)

    greet(ahead)
    greet(behind)
    greet(partner)
    for k in range(1, plane):
        greet(mate(k)[1])
    for k in range(1, nz):
        greet((lax.rem(z + k, nz), y, x, b))
    greeted = 3 + plane - 1 + nz - 1

    for d in range(3):
        xs[d, 0:side, :] = jnp.zeros((side, ch), BF16)
        xs[d, side + cells : 2 * side + cells, :] = jnp.zeros((side, ch), BF16)
    column = lax.rem(lax.broadcasted_iota(jnp.int32, (cells, ch), 0), side)
    inner_left = column != 0
    inner_right = column != side - 1
    for c in loads:
        c.wait()

    def place(value):
        xs[1, side : side + cells, :] = value.astype(BF16)
        xs[0, side : side + cells, :] = jnp.where(inner_left, pltpu.roll(value, 1, 0), 0.0).astype(BF16)
        xs[2, side : side + cells, :] = jnp.where(inner_right, pltpu.roll(value, cells - 1, 0), 0.0).astype(BF16)

    def patches():
        return jnp.concatenate(
            [xs[dx, side * dy : side * dy + cells, :] for dy in range(3) for dx in range(3)], axis=1
        )

    def activate(n, u):
        place(u)
        return jnp.tanh(dot(patches(), w[n]) + bias[pl.ds(n, 1), :])

    def adjoint_conv(n, columns):
        flipped = jnp.concatenate([w[n, ch * (8 - t) : ch * (9 - t), :] for t in range(9)], axis=1)
        return dot(columns, flipped, True)

    def relax(u):
        return lax.fori_loop(0, blocks, lambda n, s: s + STEP * activate(n, s), u)

    def back_relax(lam):
        def body(k, lam):
            n = blocks - 1 - k
            place(slopes[n] * lam)
            return lam + STEP * adjoint_conv(n, patches())

        return lax.fori_loop(0, blocks, body, lam)

    eye = (
        lax.broadcasted_iota(jnp.int32, (ch, ch), 0) == lax.broadcasted_iota(jnp.int32, (ch, ch), 1)
    ).astype(F32)
    centre = w[0, 4 * ch : 5 * ch, :]
    half = ch // nb
    mine = pl.ds(pl.multiple_of(half * b, half), half)
    other = pl.ds(pl.multiple_of(half * (1 - b), half), half)

    def mats(level, buf, index, size, to):
        def start():
            for k in range(1, size):
                copy(
                    buf.at[index, mine], buf.at[index, mine], mat_s.at[level, k], mat_r.at[level, k],
                    to(lax.rem(index + k, size)),
                ).start()

        def relay():
            for k in range(1, size):
                source = lax.rem(index - k + size, size)
                copy(
                    buf.at[source, mine], buf.at[source, mine], mat_s.at[level, k], mat_r.at[level, k], partner
                ).wait_recv()
                copy(
                    buf.at[source, mine], buf.at[source, mine], pair_s.at[level, k], pair_r.at[level, k], partner
                ).start()

        def finish():
            for k in range(1, size):
                source = lax.rem(index - k + size, size)
                copy(
                    buf.at[source, other], buf.at[source, other], pair_s.at[level, k], pair_r.at[level, k], partner
                ).wait_recv()

        def drain():
            for k in range(1, size):
                source = lax.rem(index - k + size, size)
                copy(
                    buf.at[index, mine], buf.at[index, mine], mat_s.at[level, k], mat_r.at[level, k], partner
                ).wait_send()
                copy(
                    buf.at[source, mine], buf.at[source, mine], pair_s.at[level, k], pair_r.at[level, k], partner
                ).wait_send()

        return start, relay, finish, drain

    row_mats = mats(0, kx, x, nx, lambda t: (z, y, t, b))
    column_mats = mats(1, ry, y, ny, lambda t: (z, t, x, b))
    z_mats = mats(2, pz, z, nz, lambda t: (t, y, x, b))

    kx[x] = centre.astype(F32)
    pl.semaphore_wait(barrier, greeted)
    row_mats[0]()
    relaxed = relax(states[...])
    shift_src[0] = relaxed
    forward_shift = copy(shift_src.at[0], shift_dst.at[0], shift_s.at[0], shift_r.at[0], ahead)
    forward_shift.start()

    row_mats[1]()
    row_mats[2]()
    pm[0] = eye
    for j in range(nx):
        pm[j + 1] = pm[j] + coarse_step * times_exact(pm[j], kx[j].astype(BF16))
    sm[nx - 1] = eye
    for j in range(nx - 1, 0, -1):
        sm[j - 1] = sm[j] + coarse_step * exact_times(kx[j].astype(BF16), sm[j])
    ry[y] = pm[nx]
    column_mats[0]()

    def coarse_of(field, flip):
        return field + coarse_step * times_exact(field, centre, flip)

    def scan(d, extra_up, extra_z):
        flip = d == 1
        row_later, row_sooner = (pm, sm) if flip else (sm, pm)
        column_later, column_sooner = (pr, sr) if flip else (sr, pr)
        w_src[d] = times(c_buf[d], row_later[x], flip)
        for k in range(1, plane):
            t, to = mate(k)
            piece = pl.ds(pl.multiple_of(own_cells * t, own_cells), own_cells)
            copy(w_src.at[d, piece], up.at[d, me], up_s.at[d, k], up_r.at[d, k], to).start()
        own = pl.ds(pl.multiple_of(own_cells * me, own_cells), own_cells)
        up[d, me] = w_src[d, own]

        def chain_copy():
            to = lax.rem(x + (nx - 1 if flip else 1), nx)
            return copy(v_src.at[d], v_dst.at[d], chain_s.at[d], chain_r.at[d], (z, y, to, b))

        def chain(k):
            sender = nx - 1 - k if flip else k
            if k >= nx - 1:
                return

            @pl.when(x == sender)
            def _():
                if k == 0:
                    v_src[d] = c_buf[d]
                else:
                    chain_copy().wait_recv()
                    v_src[d] = coarse_of(v_dst[d], flip) + c_buf[d]
                chain_copy().start()

        chain(0)
        extra_up()
        for k in range(1, plane):
            source = lax.rem(me - k + plane, plane)
            copy(w_src.at[d, own], up.at[d, source], up_s.at[d, k], up_r.at[d, k], partner).wait_recv()
        row_total = [sum(up[d, r * nx + i] for i in range(nx)) for r in range(ny)]
        tz[d, z] = sum(times(row_total[r], column_later[r], flip) for r in range(ny))
        for k in range(1, nz):
            to = lax.rem(z + k, nz)
            copy(tz.at[d, z], tz.at[d, z], z_s.at[d, k], z_r.at[d, k], (to, y, x, b)).start()
        inside = [None] * ny
        order = list(range(ny - 1, -1, -1)) if flip else list(range(ny))
        inside[order[0]] = jnp.zeros((own_cells, ch), F32)
        for r, s in zip(order, order[1:]):
            inside[s] = times(inside[r], ry[r], flip) + row_total[r]
        chain(1)
        extra_z()
        for k in range(1, nz):
            source = lax.rem(z - k + nz, nz)
            copy(tz.at[d, source], tz.at[d, source], z_s.at[d, k], z_r.at[d, k], partner).wait_recv()

        def advance(k, s):
            i = nz - 1 - k if flip else k
            return times(s, pz[i], flip) + tz[d, i]

        entering = lax.fori_loop(0, nz - 1 - z if flip else z, advance, jnp.zeros((own_cells, ch), F32))
        for r in range(ny):
            row_src[d, r] = times(entering, column_sooner[r], flip) + inside[r]
        for k in range(1, plane):
            t, to = mate(k)
            copy(row_src.at[d, t // nx], down.at[d, own], down_s.at[d, k], down_r.at[d, k], to).start()
        down[d, own] = row_src[d, y]
        for k in range(2, nx - 1):
            chain(k)
        for k in range(1, plane):
            source = lax.rem(me - k + plane, plane)
            piece = pl.ds(pl.multiple_of(own_cells * source, own_cells), own_cells)
            copy(row_src.at[d, y], down.at[d, piece], down_s.at[d, k], down_r.at[d, k], partner).wait_recv()
        results[d] = times(down[d], row_sooner[x], flip)

        @pl.when(x == (0 if flip else nx - 1))
        def _():
            chain_copy().wait_recv()

        @pl.when(x != (nx - 1 if flip else 0))
        def _():
            results[d] = results[d] + v_dst[d]

        def drain():
            for k in range(1, plane):
                copy(w_src.at[d, own], up.at[d, me], up_s.at[d, k], up_r.at[d, k], partner).wait_send()
                copy(row_src.at[d, y], down.at[d, own], down_s.at[d, k], down_r.at[d, k], partner).wait_send()
            for k in range(1, nz):
                copy(tz.at[d, z], tz.at[d, z], z_s.at[d, k], z_r.at[d, k], partner).wait_send()

            @pl.when(x != (0 if flip else nx - 1))
            def _():
                chain_copy().wait_send()

        return drain

    forward_shift.wait_recv()
    start = jnp.where(first, states[...], shift_dst[0])
    c_buf[0] = jnp.where(first, 0.0, -coarse_of(start, False)) + relax(start)

    def extra_up():
        column_mats[1]()
        column_mats[2]()
        pr[0] = eye
        for j in range(ny):
            pr[j + 1] = times(pr[j], ry[j])
        sr[ny - 1] = eye
        for j in range(ny - 1, 0, -1):
            sr[j - 1] = times(ry[j], sr[j])
        pz[z] = pr[ny]
        z_mats[0]()

    def extra_z():
        z_mats[1]()
        z_mats[2]()

    forward_drain = scan(0, extra_up, extra_z)
    results[0] = jnp.where(first, states[...], results[0])
    outs = [pltpu.make_async_copy(results.at[0], ns_out, out_sem.at[0])]
    outs[0].start()

    def final_step(n, u):
        u_own[n] = u
        activ = activate(n, u)
        slopes[n] = 1.0 - activ * activ
        return u + STEP * activ

    lax.fori_loop(0, blocks, final_step, results[0])
    inputs_copy = copy(u_own, u_got, u_s, u_r, partner)
    inputs_copy.start()

    shift_src[1] = back_relax(guess[...])
    back_shift = copy(shift_src.at[1], shift_dst.at[1], shift_s.at[1], shift_r.at[1], behind)
    back_shift.start()
    new_ends = jnp.where(first, 0.0, coarse_of(results[0], False)) + c_buf[0]
    v_src[2] = new_ends
    outs.append(pltpu.make_async_copy(v_src.at[2], ne_out, out_sem.at[1]))
    outs[-1].start()
    for n in range(blocks):
        xt[n] = jnp.transpose(u_own[n]).astype(BF16)
    inputs_copy.wait_recv()
    for n in range(blocks):
        xt_got[n] = jnp.transpose(u_got[n]).astype(BF16)
    back_shift.wait_recv()
    back_start = jnp.where(final, guess[...], shift_dst[1])
    c_buf[1] = jnp.where(final, 0.0, -coarse_of(back_start, True)) + back_relax(back_start)
    back_drain = scan(1, lambda: None, lambda: None)
    results[1] = jnp.where(final, guess[...], results[1])
    outs.append(pltpu.make_async_copy(results.at[1], na_out, out_sem.at[2]))
    outs[-1].start()

    def sens_copy(n):
        return copy(sens_own.at[n], sens_got.at[n], sens_s.at[n], sens_r.at[n], partner)

    def bias_sum(sens):
        return jnp.sum(sens.astype(BF16).astype(F32), axis=0, keepdims=True)

    lam_ref[...] = results[1]
    for n in range(blocks - 1, -1, -1):
        sens = slopes[n] * lam_ref[...]
        sens_own[n] = sens
        sens_copy(n).start()
        place(sens)
        columns = patches()
        if n > 0:
            lam_ref[...] = lam_ref[...] + STEP * adjoint_conv(n, columns)
        gb_sum[n : n + 1, :] = bias_sum(sens)
        g_own[n] = dot(xt[n], columns)
    new_back = jnp.where(final, 0.0, coarse_of(results[1], True)) + c_buf[1]
    v_src[3] = new_back
    outs.append(pltpu.make_async_copy(v_src.at[3], nb_out, out_sem.at[3]))
    outs[-1].start()
    factor = STEP / (nb * batch * cells)
    for n in range(blocks - 1, -1, -1):
        sens_copy(n).wait_recv()
        place(sens_got[n])
        gb_sum[n : n + 1, :] = factor * (gb_sum[n : n + 1, :] + bias_sum(sens_got[n]))
        total = factor * (g_own[n] + dot(xt_got[n], patches()))
        for t in range(9):
            g_sum[n, t] = total[:, ch * (8 - t) : ch * (9 - t)]
        outs.append(pltpu.make_async_copy(g_sum.at[n], gk_out.at[n], out_sem.at[4 + n]))
        outs[-1].start()
    outs.append(pltpu.make_async_copy(gb_sum, gb_out, out_sem.at[4 + blocks]))
    outs[-1].start()

    for n in range(blocks):
        sens_copy(n).wait_send()
    inputs_copy.wait_send()
    forward_shift.wait_send()
    back_shift.wait_send()
    row_mats[3]()
    column_mats[3]()
    z_mats[3]()
    forward_drain()
    back_drain()
    for c in outs:
        c.wait()


def flush(*refs):
    sem = refs[-1]
    copies = [pltpu.make_async_copy(refs[i], refs[6 + i], sem.at[i]) for i in range(6)]
    for c in copies:
        c.start()
    for c in copies:
        c.wait()


def body(sizes, kernels, biases, states, adjoint_guess):
    nz, ny, nx, nb = sizes
    plane = ny * nx
    blocks, taps, ch, _ = kernels.shape
    side = states.shape[2]
    batch = states.shape[1]
    cells = side * side
    own = cells // plane
    field = jax.ShapeDtypeStruct((cells, ch), F32)
    dma = pltpu.SemaphoreType.DMA
    most = max(nz, ny, nx)
    vmem = pltpu.VMEM
    scratch = [
        vmem((blocks, taps * ch, ch), BF16),
        vmem((blocks, ch), F32),
        vmem((cells, ch), F32),
        vmem((cells, ch), F32),
        vmem((3, cells + 2 * side, ch), BF16),
        vmem((blocks, ch, cells), BF16),
        vmem((blocks, cells, ch), F32),
        vmem((nx, ch, ch), F32),
        vmem((ny, ch, ch), F32),
        vmem((nz, ch, ch), F32),
        vmem((nx + 1, ch, ch), F32),
        vmem((nx, ch, ch), F32),
        vmem((ny + 1, ch, ch), F32),
        vmem((ny, ch, ch), F32),
        vmem((2, cells, ch), F32),
        vmem((2, cells, ch), F32),
        vmem((2, cells, ch), F32),
        vmem((4, cells, ch), F32),
        vmem((2, cells, ch), F32),
        vmem((2, cells, ch), F32),
        vmem((2, plane, own, ch), F32),
        vmem((2, nz, own, ch), F32),
        vmem((2, ny, own, ch), F32),
        vmem((2, cells, ch), F32),
        vmem((2, cells, ch), F32),
        vmem((cells, ch), F32),
        vmem((blocks, cells, ch), F32),
        vmem((blocks, cells, ch), F32),
        vmem((blocks, ch, cells), BF16),
        vmem((blocks, cells, ch), F32),
        vmem((blocks, cells, ch), F32),
        vmem((blocks, ch, taps * ch), F32),
        vmem((blocks, taps, ch, ch), F32),
        vmem((blocks, ch), F32),
        dma((3 + blocks,)),
        dma((5 + blocks,)),
        dma((3, most)),
        dma((3, most)),
        dma((3, most)),
        dma((3, most)),
        dma((2,)),
        dma((2,)),
        dma((2,)),
        dma((2,)),
        dma((2, plane)),
        dma((2, plane)),
        dma((2, nz)),
        dma((2, nz)),
        dma((2, plane)),
        dma((2, plane)),
        dma(()),
        dma(()),
        dma((blocks,)),
        dma((blocks,)),
    ]
    any_space = pl.BlockSpec(memory_space=pl.ANY)
    outs = pl.pallas_call(
        functools.partial(kernel, sizes, blocks, side, batch),
        out_shape=[field] * 4
        + [jax.ShapeDtypeStruct((blocks, taps, ch, ch), F32), jax.ShapeDtypeStruct((blocks, ch), F32)],
        in_specs=[pl.BlockSpec(memory_space=pltpu.HBM)] * 4,
        out_specs=[any_space] * 6,
        scratch_shapes=scratch,
        compiler_params=pltpu.CompilerParams(
            collective_id=0, has_side_effects=True, vmem_limit_bytes=40 * 1024 * 1024
        ),
        name="vcycle",
    )(
        *(
            pltpu.with_memory_space_constraint(a, pltpu.HBM)
            for a in (
                kernels.reshape(blocks, taps * ch, ch),
                biases,
                states.reshape(cells, ch),
                adjoint_guess.reshape(cells, ch),
            )
        )
    )
    outs = pl.pallas_call(
        flush,
        out_shape=[jax.ShapeDtypeStruct(out.shape, out.dtype) for out in outs],
        in_specs=[any_space] * 6,
        out_specs=[pl.BlockSpec(memory_space=pltpu.HBM)] * 6,
        scratch_shapes=[dma((6,))],
        compiler_params=pltpu.CompilerParams(vmem_limit_bytes=1024 * 1024),
        name="flush",
    )(*outs)
    fields = [out.reshape(states.shape) for out in outs[:4]]
    return (*fields, outs[4], outs[5])


def solution(mesh, sizes=(8, 4, 4)):
    sizes = (*sizes, mesh.shape["batch"])
    torus = Mesh(mesh.devices.reshape(sizes), AXES)
    state = P(LAYER, "batch", None, None, None)
    return jax.shard_map(
        functools.partial(body, sizes),
        mesh=torus,
        in_specs=(P(LAYER, None, None, None), P(LAYER, None), state, state),
        out_specs=(state, state, state, state, P(LAYER, None, None, None), P(LAYER, None)),
        check_vma=False,
    )
```

```python
import functools

import jax
import jax.numpy as jnp
from jax import lax
from jax.experimental import pallas as pl
from jax.experimental.pallas import tpu as pltpu
from jax.sharding import Mesh
from jax.sharding import PartitionSpec as P

LAYER = ("layer_0", "layer_1", "layer_2")
AXES = LAYER + ("batch",)
MESH = pl.DeviceIdType.MESH
STEP = 0.1
F32 = jnp.float32
BF16 = jnp.bfloat16


def split(value):
    high = value.astype(BF16)
    return high, (value - high.astype(F32)).astype(BF16)


def dot(left, right, flip=False):
    contract = (((1,), (1,)), ((), ())) if flip else (((1,), (0,)), ((), ()))
    return lax.dot_general(left, right, contract, preferred_element_type=F32)


def times_exact(left, exact, flip=False):
    high, low = split(left)
    return dot(high, exact, flip) + dot(low, exact, flip)


def exact_times(exact, right):
    high, low = split(right)
    return dot(exact, high) + dot(exact, low)


def times(left, right, flip=False):
    high, low = split(left)
    right_high, right_low = split(right)
    return dot(high, right_high, flip) + (dot(low, right_high, flip) + dot(high, right_low, flip))


def kernel(
    sizes, blocks, side, batch,
    k_hbm, b_hbm, st_hbm, ad_hbm,
    ns_out, ne_out, na_out, nb_out, gk_out, gb_out,
    w, bias, states, guess, middle,
    xs, xt, slopes,
    kx, ry, pz, pm, sm, pr, sr,
    shift_src, shift_dst, c_buf, v_src, v_dst,
    w_src, up, tz, row_src, down, results, lam_ref,
    u_own, u_got, xt_got, sens_own, sens_got, g_own, g_sum, gb_sum,
    in_sem, out_sem,
    mat_s, mat_r, pair_s, pair_r,
    shift_s, shift_r, chain_s, chain_r,
    up_s, up_r, z_s, z_r, down_s, down_r,
    u_s, u_r, sens_s, sens_r,
):
    nz, ny, nx, nb = sizes
    plane = ny * nx
    ch = w.shape[-1]
    cells = side * side
    own_cells = cells // plane
    coarse_step = blocks * STEP
    z, y, x = (lax.axis_index(a) for a in LAYER)
    b = lax.axis_index("batch")
    me = y * nx + x
    pos = z * plane + me
    last = nz * plane - 1
    first = pos == 0
    final = pos == last

    def device(position):
        return (position // plane, lax.rem(position // nx, ny), lax.rem(position, nx), b)

    ahead = device(lax.rem(pos + 1, last + 1))
    behind = device(lax.rem(pos + last, last + 1))
    partner = (z, y, x, 1 - b)

    def ring(step, size):
        return min(step, size - step)

    offsets = sorted(
        ((dy, dx) for dy in range(ny) for dx in range(nx) if dy or dx),
        key=lambda o: -ring(o[0], ny) - ring(o[1], nx),
    )
    z_steps = sorted(range(1, nz), key=lambda k: -ring(k, nz))

    def mate(offset):
        ty, tx = lax.rem(y + offset[0], ny), lax.rem(x + offset[1], nx)
        return ty, ty * nx + tx, (z, ty, tx, b)

    def copy(src, dst, send, recv, to):
        return pltpu.make_async_remote_copy(
            src_ref=src, dst_ref=dst, send_sem=send, recv_sem=recv, device_id=to, device_id_type=MESH
        )

    loads = [
        pltpu.make_async_copy(k_hbm.at[0, 4 * ch : 5 * ch], middle, in_sem.at[0]),
        pltpu.make_async_copy(st_hbm, states, in_sem.at[1]),
        pltpu.make_async_copy(b_hbm, bias, in_sem.at[2]),
        pltpu.make_async_copy(k_hbm, w, in_sem.at[3]),
        pltpu.make_async_copy(ad_hbm, guess, in_sem.at[4]),
    ]
    for c in loads:
        c.start()

    barrier = pltpu.get_barrier_semaphore()

    def greet(to):
        pl.semaphore_signal(barrier, inc=1, device_id=to, device_id_type=MESH)

    greet(ahead)
    greet(behind)
    greet(partner)
    for o in offsets:
        greet(mate(o)[2])
    for k in range(1, nz):
        greet((lax.rem(z + k, nz), y, x, b))
    greeted = 3 + plane - 1 + nz - 1

    for d in range(3):
        xs[d, 0:side, :] = jnp.zeros((side, ch), BF16)
        xs[d, side + cells : 2 * side + cells, :] = jnp.zeros((side, ch), BF16)
    column = lax.rem(lax.broadcasted_iota(jnp.int32, (cells, ch), 0), side)
    inner_left = column != 0
    inner_right = column != side - 1

    def place(value):
        xs[1, side : side + cells, :] = value.astype(BF16)
        xs[0, side : side + cells, :] = jnp.where(inner_left, pltpu.roll(value, 1, 0), 0.0).astype(BF16)
        xs[2, side : side + cells, :] = jnp.where(inner_right, pltpu.roll(value, cells - 1, 0), 0.0).astype(BF16)

    def patches():
        return jnp.concatenate(
            [xs[dx, side * dy : side * dy + cells, :] for dy in range(3) for dx in range(3)], axis=1
        )

    def activate(n, u):
        place(u)
        return jnp.tanh(dot(patches(), w[n]) + bias[pl.ds(n, 1), :])

    def adjoint_conv(n, columns):
        flipped = jnp.concatenate([w[n, ch * (8 - t) : ch * (9 - t), :] for t in range(9)], axis=1)
        return dot(columns, flipped, True)

    def relax(u):
        return lax.fori_loop(0, blocks, lambda n, s: s + STEP * activate(n, s), u)

    def back_relax(lam):
        def body(k, lam):
            n = blocks - 1 - k
            place(slopes[n] * lam)
            return lam + STEP * adjoint_conv(n, patches())

        return lax.fori_loop(0, blocks, body, lam)

    eye = (
        lax.broadcasted_iota(jnp.int32, (ch, ch), 0) == lax.broadcasted_iota(jnp.int32, (ch, ch), 1)
    ).astype(F32)
    half = ch // nb
    mine = pl.ds(pl.multiple_of(half * b, half), half)
    other = pl.ds(pl.multiple_of(half * (1 - b), half), half)

    def mats(level, buf, index, size, to):
        near = [k for k in range(1, size) if ring(k, size) <= 2]
        near.sort(key=lambda k: -ring(k, size))
        far = [k for k in range(1, size) if ring(k, size) > 2]

        def from_step(k):
            return lax.rem(index - k + size, size)

        def move(source, k, target):
            return copy(
                buf.at[source, mine], buf.at[source, mine], mat_s.at[level], mat_r.at[level, k], target
            )

        def swap(source):
            return copy(buf.at[source, mine], buf.at[source, mine], pair_s.at[level], pair_r.at[level], partner)

        def start():
            for k in near:
                move(index, k, to(lax.rem(index + k, size))).start()

        def relay():
            for k in near:
                source = from_step(k)
                move(source, k, partner).wait_recv()
                for f in far:
                    through = 2 if f <= size // 2 else size - 2
                    if k == through:
                        move(source, f, to(lax.rem(index + f - k + size, size))).start()
                swap(source).start()
            for f in far:
                source = from_step(f)
                move(source, f, partner).wait_recv()
                swap(source).start()

        def all_of():
            return buf.at[0 : size - 1, mine]

        def finish():
            if size > 1:
                copy(all_of(), all_of(), pair_s.at[level], pair_r.at[level], partner).wait_recv()

        def drain():
            if size > 1:
                copy(all_of(), all_of(), mat_s.at[level], pair_r.at[level], partner).wait_send()
                copy(all_of(), all_of(), pair_s.at[level], pair_r.at[level], partner).wait_send()

        return start, relay, finish, drain

    row_mats = mats(0, kx, x, nx, lambda t: (z, y, t, b))
    column_mats = mats(1, ry, y, ny, lambda t: (z, t, x, b))
    z_mats = mats(2, pz, z, nz, lambda t: (t, y, x, b))

    loads[0].wait()
    kx[x] = middle[...].astype(F32)
    pl.semaphore_wait(barrier, greeted)
    row_mats[0]()
    for c in loads[1:]:
        c.wait()
    relaxed = relax(states[...])
    shift_src[0] = relaxed
    forward_shift = copy(shift_src.at[0], shift_dst.at[0], shift_s.at[0], shift_r.at[0], ahead)
    forward_shift.start()

    row_mats[1]()
    row_mats[2]()
    def step_map(j):
        return eye + coarse_step * kx[j]

    middle_x = (nx + 1) // 2
    pm[0] = eye
    sm[nx - 1] = eye

    def row_sooner_map(j):
        pm[j] = step_map(0) if j == 1 else pm[j - 1] + coarse_step * times_exact(pm[j - 1], kx[j - 1].astype(BF16))

    def row_later_map(j):
        first_later = step_map(j + 1)
        sm[j] = first_later if j == nx - 2 else sm[j + 1] + coarse_step * exact_times(kx[j + 1].astype(BF16), sm[j + 1])

    for j in range(1, middle_x + 1):
        row_sooner_map(j)
    for j in range(nx - 2, middle_x - 2, -1):
        row_later_map(j)
    ry[y] = times(pm[middle_x], sm[middle_x - 1]) if nx > 1 else pm[1]
    column_mats[0]()
    for j in range(middle_x + 1, nx):
        row_sooner_map(j)
    for j in range(middle_x - 2, -1, -1):
        row_later_map(j)

    def coarse_of(field, flip):
        return field + coarse_step * times_exact(field, middle[...], flip)

    def scan(d, extra_up, extra_z):
        flip = d == 1
        row_later, row_sooner = (pm, sm) if flip else (sm, pm)
        column_later, column_sooner = (pr, sr) if flip else (sr, pr)
        w_src[d] = times(c_buf[d], row_later[x], flip)
        for o in offsets:
            _, t, to = mate(o)
            piece = pl.ds(pl.multiple_of(own_cells * t, own_cells), own_cells)
            copy(w_src.at[d, piece], up.at[d, me], up_s.at[d], up_r.at[d], to).start()
        own = pl.ds(pl.multiple_of(own_cells * me, own_cells), own_cells)
        up[d, me] = w_src[d, own]

        def chain_copy():
            to = lax.rem(x + (nx - 1 if flip else 1), nx)
            return copy(v_src.at[d], v_dst.at[d], chain_s.at[d], chain_r.at[d], (z, y, to, b))

        def chain(k):
            sender = nx - 1 - k if flip else k
            if k >= nx - 1:
                return

            @pl.when(x == sender)
            def _():
                if k == 0:
                    v_src[d] = c_buf[d]
                else:
                    chain_copy().wait_recv()
                    v_src[d] = coarse_of(v_dst[d], flip) + c_buf[d]
                chain_copy().start()

        chain(0)
        extra_up()
        pieces = up.at[d, 0 : plane - 1]
        if plane > 1:
            copy(pieces, pieces, up_s.at[d], up_r.at[d], partner).wait_recv()
        row_total = [sum(up[d, r * nx + i] for i in range(nx)) for r in range(ny)]
        tz[d, z] = sum(times(row_total[r], column_later[r], flip) for r in range(ny))
        for k in z_steps:
            to = lax.rem(z + k, nz)
            copy(tz.at[d, z], tz.at[d, z], z_s.at[d], z_r.at[d], (to, y, x, b)).start()
        inside = [None] * ny
        order = list(range(ny - 1, -1, -1)) if flip else list(range(ny))
        inside[order[0]] = jnp.zeros((own_cells, ch), F32)
        for r, s in zip(order, order[1:]):
            inside[s] = times(inside[r], ry[r], flip) + row_total[r]
        chain(1)
        extra_z()
        totals = tz.at[d, 0 : nz - 1]
        copy(totals, totals, z_s.at[d], z_r.at[d], partner).wait_recv()

        def advance(k, s):
            i = nz - 1 - k if flip else k
            return times(s, pz[i], flip) + tz[d, i]

        entering = lax.fori_loop(0, nz - 1 - z if flip else z, advance, jnp.zeros((own_cells, ch), F32))
        for r in range(ny):
            row_src[d, r] = times(entering, column_sooner[r], flip) + inside[r]
        for o in offsets:
            ty, _, to = mate(o)
            copy(row_src.at[d, ty], down.at[d, own], down_s.at[d], down_r.at[d], to).start()
        down[d, own] = row_src[d, y]
        for k in range(2, nx - 1):
            chain(k)
        if plane > 1:
            copy(pieces, pieces, down_s.at[d], down_r.at[d], partner).wait_recv()
        results[d] = times(down[d], row_sooner[x], flip)

        if nx > 1:

            @pl.when(x == (0 if flip else nx - 1))
            def _():
                chain_copy().wait_recv()

            @pl.when(x != (nx - 1 if flip else 0))
            def _():
                results[d] = results[d] + v_dst[d]

        def drain():
            if plane > 1:
                copy(pieces, pieces, up_s.at[d], up_r.at[d], partner).wait_send()
                copy(pieces, pieces, down_s.at[d], down_r.at[d], partner).wait_send()
            copy(totals, totals, z_s.at[d], z_r.at[d], partner).wait_send()

            if nx > 1:

                @pl.when(x != (0 if flip else nx - 1))
                def _():
                    chain_copy().wait_send()

        return drain

    forward_shift.wait_recv()
    start = jnp.where(first, states[...], shift_dst[0])
    c_buf[0] = jnp.where(first, 0.0, -coarse_of(start, False)) + relax(start)

    def extra_up():
        column_mats[1]()
        column_mats[2]()
        middle_y = (ny + 1) // 2
        pr[0] = eye
        sr[ny - 1] = eye

        def sooner(j):
            pr[j] = ry[0] if j == 1 else times(pr[j - 1], ry[j - 1])

        def later(j):
            sr[j] = ry[j + 1] if j == ny - 2 else times(ry[j + 1], sr[j + 1])

        for j in range(1, middle_y + 1):
            sooner(j)
        for j in range(ny - 2, middle_y - 2, -1):
            later(j)
        pz[z] = times(pr[middle_y], sr[middle_y - 1]) if ny > 1 else pr[1]
        z_mats[0]()
        for j in range(middle_y + 1, ny):
            sooner(j)
        for j in range(middle_y - 2, -1, -1):
            later(j)

    def extra_z():
        z_mats[1]()
        z_mats[2]()

    forward_drain = scan(0, extra_up, extra_z)
    results[0] = jnp.where(first, states[...], results[0])
    pltpu.make_async_copy(results.at[0], ns_out, out_sem.at[0]).start()

    def final_step(n, u):
        u_own[n] = u
        activ = activate(n, u)
        slopes[n] = 1.0 - activ * activ
        return u + STEP * activ

    lax.fori_loop(0, blocks, final_step, results[0])
    inputs_copy = copy(u_own, u_got, u_s, u_r, partner)
    inputs_copy.start()

    shift_src[1] = back_relax(guess[...])
    back_shift = copy(shift_src.at[1], shift_dst.at[1], shift_s.at[1], shift_r.at[1], behind)
    back_shift.start()
    new_ends = jnp.where(first, 0.0, coarse_of(results[0], False)) + c_buf[0]
    v_src[2] = new_ends
    pltpu.make_async_copy(v_src.at[2], ne_out, out_sem.at[0]).start()
    for n in range(blocks):
        xt[n] = jnp.transpose(u_own[n]).astype(BF16)
    inputs_copy.wait_recv()
    for n in range(blocks):
        xt_got[n] = jnp.transpose(u_got[n]).astype(BF16)
    back_shift.wait_recv()
    back_start = jnp.where(final, guess[...], shift_dst[1])
    c_buf[1] = jnp.where(final, 0.0, -coarse_of(back_start, True)) + back_relax(back_start)
    back_drain = scan(1, lambda: None, lambda: None)
    results[1] = jnp.where(final, guess[...], results[1])
    pltpu.make_async_copy(results.at[1], na_out, out_sem.at[0]).start()

    def sens_copy(n):
        return copy(sens_own.at[n], sens_got.at[n], sens_s, sens_r.at[n], partner)

    def bias_sum(sens):
        return jnp.sum(sens.astype(BF16).astype(F32), axis=0, keepdims=True)

    lam_ref[...] = results[1]
    for n in range(blocks - 1, -1, -1):
        sens = slopes[n] * lam_ref[...]
        sens_own[n] = sens
        sens_copy(n).start()
        place(sens)
        columns = patches()
        if n > 0:
            lam_ref[...] = lam_ref[...] + STEP * adjoint_conv(n, columns)
        gb_sum[n : n + 1, :] = bias_sum(sens)
        g_own[n] = dot(xt[n], columns)
    new_back = jnp.where(final, 0.0, coarse_of(results[1], True)) + c_buf[1]
    v_src[3] = new_back
    pltpu.make_async_copy(v_src.at[3], nb_out, out_sem.at[0]).start()
    factor = STEP / (nb * batch * cells)
    for n in range(blocks - 1, -1, -1):
        sens_copy(n).wait_recv()
        place(sens_got[n])
        gb_sum[n : n + 1, :] = factor * (gb_sum[n : n + 1, :] + bias_sum(sens_got[n]))
        total = factor * (g_own[n] + dot(xt_got[n], patches()))
        for t in range(9):
            g_sum[n, t] = total[:, ch * (8 - t) : ch * (9 - t)]
        pltpu.make_async_copy(g_sum.at[n], gk_out.at[n], out_sem.at[1]).start()
    bias_out = pltpu.make_async_copy(gb_sum, gb_out, out_sem.at[2])
    bias_out.start()

    copy(sens_own, sens_got, sens_s, u_r, partner).wait_send()
    inputs_copy.wait_send()
    forward_shift.wait_send()
    back_shift.wait_send()
    row_mats[3]()
    column_mats[3]()
    z_mats[3]()
    forward_drain()
    back_drain()
    pltpu.make_async_copy(v_src, v_src, out_sem.at[0]).wait()
    pltpu.make_async_copy(g_sum, gk_out, out_sem.at[1]).wait()
    bias_out.wait()


def flush(*refs):
    sem = refs[-1]
    copies = [pltpu.make_async_copy(refs[i], refs[6 + i], sem.at[i]) for i in range(6)]
    for c in copies:
        c.start()
    for c in copies:
        c.wait()


def body(sizes, kernels, biases, states, adjoint_guess):
    nz, ny, nx, nb = sizes
    plane = ny * nx
    blocks, taps, ch, _ = kernels.shape
    side = states.shape[2]
    batch = states.shape[1]
    cells = side * side
    own = cells // plane
    field = jax.ShapeDtypeStruct((cells, ch), F32)
    dma = pltpu.SemaphoreType.DMA
    most = max(nz, ny, nx)
    vmem = pltpu.VMEM
    scratch = [
        vmem((blocks, taps * ch, ch), BF16),
        vmem((blocks, ch), F32),
        vmem((cells, ch), F32),
        vmem((cells, ch), F32),
        vmem((ch, ch), BF16),
        vmem((3, cells + 2 * side, ch), BF16),
        vmem((blocks, ch, cells), BF16),
        vmem((blocks, cells, ch), F32),
        vmem((nx, ch, ch), F32),
        vmem((ny, ch, ch), F32),
        vmem((nz, ch, ch), F32),
        vmem((nx + 1, ch, ch), F32),
        vmem((nx, ch, ch), F32),
        vmem((ny + 1, ch, ch), F32),
        vmem((ny, ch, ch), F32),
        vmem((2, cells, ch), F32),
        vmem((2, cells, ch), F32),
        vmem((2, cells, ch), F32),
        vmem((4, cells, ch), F32),
        vmem((2, cells, ch), F32),
        vmem((2, cells, ch), F32),
        vmem((2, plane, own, ch), F32),
        vmem((2, nz, own, ch), F32),
        vmem((2, ny, own, ch), F32),
        vmem((2, cells, ch), F32),
        vmem((2, cells, ch), F32),
        vmem((cells, ch), F32),
        vmem((blocks, cells, ch), F32),
        vmem((blocks, cells, ch), F32),
        vmem((blocks, ch, cells), BF16),
        vmem((blocks, cells, ch), F32),
        vmem((blocks, cells, ch), F32),
        vmem((blocks, ch, taps * ch), F32),
        vmem((blocks, taps, ch, ch), F32),
        vmem((blocks, ch), F32),
        dma((5,)),
        dma((3,)),
        dma((3,)),
        dma((3, most)),
        dma((3,)),
        dma((3,)),
        dma((2,)),
        dma((2,)),
        dma((2,)),
        dma((2,)),
        dma((2,)),
        dma((2,)),
        dma((2,)),
        dma((2,)),
        dma((2,)),
        dma((2,)),
        dma(()),
        dma(()),
        dma(()),
        dma((blocks,)),
    ]
    any_space = pl.BlockSpec(memory_space=pl.ANY)
    outs = pl.pallas_call(
        functools.partial(kernel, sizes, blocks, side, batch),
        out_shape=[field] * 4
        + [jax.ShapeDtypeStruct((blocks, taps, ch, ch), F32), jax.ShapeDtypeStruct((blocks, ch), F32)],
        in_specs=[pl.BlockSpec(memory_space=pltpu.HBM)] * 4,
        out_specs=[any_space] * 6,
        scratch_shapes=scratch,
        compiler_params=pltpu.CompilerParams(
            collective_id=0, has_side_effects=True, vmem_limit_bytes=40 * 1024 * 1024
        ),
        name="vcycle",
    )(
        *(
            pltpu.with_memory_space_constraint(a, pltpu.HBM)
            for a in (
                kernels.reshape(blocks, taps * ch, ch),
                biases,
                states.reshape(cells, ch),
                adjoint_guess.reshape(cells, ch),
            )
        )
    )
    outs = pl.pallas_call(
        flush,
        out_shape=[jax.ShapeDtypeStruct(out.shape, out.dtype) for out in outs],
        in_specs=[any_space] * 6,
        out_specs=[pl.BlockSpec(memory_space=pltpu.HBM)] * 6,
        scratch_shapes=[dma((6,))],
        compiler_params=pltpu.CompilerParams(vmem_limit_bytes=1024 * 1024),
        name="flush",
    )(*outs)
    fields = [out.reshape(states.shape) for out in outs[:4]]
    return (*fields, outs[4], outs[5])


def solution(mesh, sizes=(8, 4, 4)):
    sizes = (*sizes, mesh.shape["batch"])
    torus = Mesh(mesh.devices.reshape(sizes), AXES)
    state = P(LAYER, "batch", None, None, None)
    return jax.shard_map(
        functools.partial(body, sizes),
        mesh=torus,
        in_specs=(P(LAYER, None, None, None), P(LAYER, None), state, state),
        out_specs=(state, state, state, state, P(LAYER, None, None, None), P(LAYER, None)),
        check_vma=False,
    )
```

```python
import functools

import jax
import jax.numpy as jnp
from jax import lax
from jax.experimental import pallas as pl
from jax.experimental.pallas import tpu as pltpu
from jax.sharding import Mesh
from jax.sharding import PartitionSpec as P

LAYER = ("layer_0", "layer_1", "layer_2")
AXES = LAYER + ("batch",)
MESH = pl.DeviceIdType.MESH
STEP = 0.1
F32 = jnp.float32
BF16 = jnp.bfloat16


def split(value):
    high = value.astype(BF16)
    return high, (value - high.astype(F32)).astype(BF16)


def dot(left, right, flip=False):
    contract = (((1,), (1,)), ((), ())) if flip else (((1,), (0,)), ((), ()))
    return lax.dot_general(left, right, contract, preferred_element_type=F32)


def times_exact(left, exact, flip=False):
    high, low = split(left)
    return dot(high, exact, flip) + dot(low, exact, flip)


def exact_times(exact, right):
    high, low = split(right)
    return dot(exact, high) + dot(exact, low)


def times(left, right, flip=False):
    high, low = split(left)
    right_high, right_low = split(right)
    return dot(high, right_high, flip) + (dot(low, right_high, flip) + dot(high, right_low, flip))


def kernel(
    sizes, blocks, side, batch,
    k_hbm, b_hbm, st_hbm, ad_hbm,
    ns_out, ne_out, na_out, nb_out, gk_out, gb_out,
    w, bias, states, guess, middle,
    xs, xt, slopes,
    kx, ry, pz, pm, sm, pr, sr,
    shift_src, shift_dst, c_buf, v_src, v_dst,
    w_src, up, tz, entering, row_src, down, results, lam_ref,
    u_own, u_got, xt_got, sens_own, sens_got, g_own, g_sum, gb_sum,
    in_sem, out_sem,
    mat_s, x_r, xp_r, y_r, yp_r, zm_r, zp_r,
    shift_s, shift_r, chain_s, chain_r,
    up_s, up_r, z_s, z_r, down_s, down_r,
    u_s, u_r, sens_s, sens_r,
):
    nz, ny, nx, nb = sizes
    plane = ny * nx
    ch = w.shape[-1]
    cells = side * side
    own_cells = cells // plane
    coarse_step = blocks * STEP
    z, y, x = (lax.axis_index(a) for a in LAYER)
    b = lax.axis_index("batch")
    me = y * nx + x
    pos = z * plane + me
    last = nz * plane - 1
    first = pos == 0
    final = pos == last

    def device(position):
        return (position // plane, lax.rem(position // nx, ny), lax.rem(position, nx), b)

    ahead = device(lax.rem(pos + 1, last + 1))
    behind = device(lax.rem(pos + last, last + 1))
    partner = (z, y, x, 1 - b)

    def ring(step, size):
        return min(step, size - step)

    offsets = sorted(
        ((dy, dx) for dy in range(ny) for dx in range(nx) if dy or dx),
        key=lambda o: -ring(o[0], ny) - ring(o[1], nx),
    )
    z_steps = sorted(range(1, nz), key=lambda k: -ring(k, nz))

    def mate(offset):
        ty, tx = lax.rem(y + offset[0], ny), lax.rem(x + offset[1], nx)
        return ty, ty * nx + tx, (z, ty, tx, b)

    def copy(src, dst, send, recv, to):
        return pltpu.make_async_remote_copy(
            src_ref=src, dst_ref=dst, send_sem=send, recv_sem=recv, device_id=to, device_id_type=MESH
        )

    loads = [
        pltpu.make_async_copy(k_hbm.at[0, 4 * ch : 5 * ch], middle, in_sem.at[0]),
        pltpu.make_async_copy(st_hbm, states, in_sem.at[1]),
        pltpu.make_async_copy(b_hbm, bias, in_sem.at[2]),
        pltpu.make_async_copy(k_hbm, w, in_sem.at[3]),
        pltpu.make_async_copy(ad_hbm, guess, in_sem.at[4]),
    ]
    for c in loads:
        c.start()

    barrier = pltpu.get_barrier_semaphore()

    def greet(to):
        pl.semaphore_signal(barrier, inc=1, device_id=to, device_id_type=MESH)

    greet(ahead)
    greet(behind)
    greet(partner)
    for o in offsets:
        greet(mate(o)[2])
    for k in range(1, nz):
        greet((lax.rem(z + k, nz), y, x, b))
    greeted = 3 + plane - 1 + nz - 1

    xs[0:side, :] = jnp.zeros((side, ch), BF16)
    xs[side + cells : 2 * side + cells, :] = jnp.zeros((side, ch), BF16)
    column = lax.rem(lax.broadcasted_iota(jnp.int32, (cells, ch), 0), side)
    inner_left = column != 0
    inner_right = column != side - 1

    def place(value):
        xs[side : side + cells, :] = value.astype(BF16)

    def rows_beside():
        return [xs[side * dy : side * dy + cells, :] for dy in range(3)]

    def from_left(value):
        return jnp.where(inner_left, pltpu.roll(value, 1, 0), 0.0)

    def from_right(value):
        return jnp.where(inner_right, pltpu.roll(value, cells - 1, 0), 0.0)

    def join_columns(wide):
        return wide[:, ch : 2 * ch] + (from_left(wide[:, :ch]) + from_right(wide[:, 2 * ch :]))

    def tap(n, t):
        return w[n, ch * t : ch * (t + 1), :]

    def activate(n, u):
        place(u)
        weights = jnp.concatenate(
            [jnp.concatenate([tap(n, 3 * dy + dx) for dx in range(3)], axis=1) for dy in range(3)], axis=0
        )
        wide = dot(jnp.concatenate(rows_beside(), axis=1), weights)
        return jnp.tanh(join_columns(wide) + bias[pl.ds(n, 1), :])

    def adjoint_conv(n):
        flipped = jnp.concatenate(
            [jnp.concatenate([tap(n, 8 - 3 * dy - dx) for dy in range(3)], axis=1) for dx in range(3)], axis=0
        )
        return join_columns(dot(jnp.concatenate(rows_beside(), axis=1), flipped, True))

    def grad_product(inputs):
        return dot(inputs, jnp.concatenate(rows_beside()[::-1], axis=1))

    def beside(u):
        return jnp.concatenate([jnp.transpose(v).astype(BF16) for v in (from_left(u), u, from_right(u))], axis=0)

    def relax(u):
        return lax.fori_loop(0, blocks, lambda n, s: s + STEP * activate(n, s), u)

    def back_relax(lam):
        def body(k, lam):
            n = blocks - 1 - k
            place(slopes[n] * lam)
            return lam + STEP * adjoint_conv(n)

        return lax.fori_loop(0, blocks, body, lam)

    eye = (
        lax.broadcasted_iota(jnp.int32, (ch, ch), 0) == lax.broadcasted_iota(jnp.int32, (ch, ch), 1)
    ).astype(F32)
    half = ch // nb
    mine = pl.ds(pl.multiple_of(half * b, half), half)
    other = pl.ds(pl.multiple_of(half * (1 - b), half), half)

    class Maps:
        def __init__(self, buf, index, size, to, send, recv, pair_send, pair_recv):
            self.buf, self.index, self.size, self.to = buf, index, size, to
            self.send, self.recv, self.pair_send, self.pair_recv = send, recv, pair_send, pair_recv
            near = [k for k in range(1, size) if ring(k, size) <= 2]
            near.sort(key=lambda k: -ring(k, size))
            far = [k for k in range(size - 1, 0, -1) if ring(k, size) > 2]
            self.near, self.far = near, far

        def source(self, k):
            return lax.rem(self.index - k + self.size, self.size)

        def move(self, source, k, target):
            part = self.buf.at[source, mine]
            return copy(part, part, self.send, self.recv.at[k], target)

        def swap(self, source, k, rows):
            part = self.buf.at[source, rows]
            return copy(part, part, self.pair_send, self.pair_recv.at[k], partner)

        def start(self):
            for k in self.near:
                self.move(self.index, k, self.to(lax.rem(self.index + k, self.size))).start()

        def pass_on(self, wanted=None, near=True, far=True):
            for k in (self.near if near else []) + (self.far if far else []):
                source = self.source(k)

                def take(k=k, source=source):
                    self.move(source, k, partner).wait_recv()
                    for f in self.far:
                        if k == (2 if f <= self.size // 2 else self.size - 2):
                            self.move(source, f, self.to(lax.rem(self.index + f - k + self.size, self.size))).start()
                    self.swap(source, k, mine).start()

                if wanted is None:
                    take()
                else:
                    pl.when(wanted(k, source))(take)

        def finish(self):
            for k in range(1, self.size):
                self.swap(self.source(k), k, other).wait_recv()

        def drain(self):
            if self.size > 1:
                part = self.buf.at[0 : self.size - 1, mine]
                copy(part, part, self.send, self.recv.at[0], partner).wait_send()
                copy(part, part, self.pair_send, self.recv.at[0], partner).wait_send()

    row_mats = Maps(kx, x, nx, lambda t: (z, y, t, b), mat_s.at[0], x_r, mat_s.at[1], xp_r)
    column_mats = Maps(ry, y, ny, lambda t: (z, t, x, b), mat_s.at[2], y_r, mat_s.at[3], yp_r)
    z_mats = Maps(pz, z, nz, lambda t: (t, y, x, b), mat_s.at[4], zm_r, mat_s.at[5], zp_r)

    loads[0].wait()
    kx[x] = middle[...].astype(F32)
    pl.semaphore_wait(barrier, greeted)
    row_mats.start()
    for c in loads[1:]:
        c.wait()
    relaxed = relax(states[...])
    shift_src[0] = relaxed
    forward_shift = copy(shift_src.at[0], shift_dst.at[0], shift_s.at[0], shift_r.at[0], ahead)
    forward_shift.start()

    row_mats.pass_on()
    row_mats.finish()
    def step_map(j):
        return eye + coarse_step * kx[j]

    middle_x = (nx + 1) // 2
    pm[0] = eye
    sm[nx - 1] = eye

    def row_sooner_map(j):
        pm[j] = step_map(0) if j == 1 else pm[j - 1] + coarse_step * times_exact(pm[j - 1], kx[j - 1].astype(BF16))

    def row_later_map(j):
        first_later = step_map(j + 1)
        sm[j] = first_later if j == nx - 2 else sm[j + 1] + coarse_step * exact_times(kx[j + 1].astype(BF16), sm[j + 1])

    for j in range(1, middle_x + 1):
        row_sooner_map(j)
    for j in range(nx - 2, middle_x - 2, -1):
        row_later_map(j)
    ry[y] = times(pm[middle_x], sm[middle_x - 1]) if nx > 1 else pm[1]
    column_mats.start()
    for j in range(middle_x + 1, nx):
        row_sooner_map(j)
    for j in range(middle_x - 2, -1, -1):
        row_later_map(j)

    def early(k, source):
        needed = (source < z) & (source != 0)
        return needed | (z == 0) if k == nz - 2 and nz > 4 else needed

    def late(k, source):
        return jnp.logical_not(early(k, source))

    def coarse_of(field, flip):
        return field + coarse_step * times_exact(field, middle[...], flip)

    def scan(d, extra_up):
        flip = d == 1
        row_later, row_sooner = (pm, sm) if flip else (sm, pm)
        column_later, column_sooner = (pr, sr) if flip else (sr, pr)
        w_src[d] = times(c_buf[d], row_later[x], flip)
        for o in offsets:
            _, t, to = mate(o)
            piece = pl.ds(pl.multiple_of(own_cells * t, own_cells), own_cells)
            copy(w_src.at[d, piece], up.at[d, me], up_s.at[d], up_r.at[d], to).start()
        own = pl.ds(pl.multiple_of(own_cells * me, own_cells), own_cells)
        up[d, me] = w_src[d, own]

        def chain_copy():
            to = lax.rem(x + (nx - 1 if flip else 1), nx)
            return copy(v_src.at[d], v_dst.at[d], chain_s.at[d], chain_r.at[d], (z, y, to, b))

        def chain(k):
            sender = nx - 1 - k if flip else k
            if k >= nx - 1:
                return

            @pl.when(x == sender)
            def _():
                if k == 0:
                    v_src[d] = c_buf[d]
                else:
                    chain_copy().wait_recv()
                    v_src[d] = coarse_of(v_dst[d], flip) + c_buf[d]
                chain_copy().start()

        chain(0)
        extra_up()
        pieces = up.at[d, 0 : plane - 1]
        if plane > 1:
            copy(pieces, pieces, up_s.at[d], up_r.at[d], partner).wait_recv()
        row_total = [sum(up[d, r * nx + i] for i in range(nx)) for r in range(ny)]
        tz[d, z] = sum(times(row_total[r], column_later[r], flip) for r in range(ny))
        for k in z_steps:
            to = lax.rem(z + k, nz)
            copy(tz.at[d, z], tz.at[d, z], z_s.at[d], z_r.at[d, k], (to, y, x, b)).start()
        inside = [None] * ny
        order = list(range(ny - 1, -1, -1)) if flip else list(range(ny))
        inside[order[0]] = jnp.zeros((own_cells, ch), F32)
        for r, s in zip(order, order[1:]):
            inside[s] = times(inside[r], ry[r], flip) + row_total[r]
        chain(1)
        if not flip:
            z_mats.pass_on(early)

        def total_from(k):
            source = lax.rem(z - k + nz, nz)
            return copy(tz.at[d, source], tz.at[d, source], z_s.at[d], z_r.at[d, k], partner)

        entering[...] = jnp.zeros((own_cells, ch), F32)
        for i in range(nz - 1, 0, -1) if flip else range(nz - 1):

            @pl.when(z < i if flip else z > i)
            def _():
                k = lax.rem(z - i + nz, nz)
                total_from(k).wait_recv()
                if i == (nz - 1 if flip else 0):
                    entering[...] = tz[d, i]
                else:
                    z_mats.swap(i, k, other).wait_recv()
                    entering[...] = times(entering[...], pz[i], flip) + tz[d, i]

        for r in range(ny):
            row_src[d, r] = times(entering[...], column_sooner[r], flip) + inside[r]
        for o in offsets:
            ty, _, to = mate(o)
            copy(row_src.at[d, ty], down.at[d, own], down_s.at[d], down_r.at[d], to).start()
        down[d, own] = row_src[d, y]
        for k in range(2, nx - 1):
            chain(k)
        if not flip:
            z_mats.pass_on(late, far=False)
        if plane > 1:
            copy(pieces, pieces, down_s.at[d], down_r.at[d], partner).wait_recv()
        results[d] = times(down[d], row_sooner[x], flip)

        if nx > 1:

            @pl.when(x == (0 if flip else nx - 1))
            def _():
                chain_copy().wait_recv()

            @pl.when(x != (nx - 1 if flip else 0))
            def _():
                results[d] = results[d] + v_dst[d]

        def drain():
            if plane > 1:
                copy(pieces, pieces, up_s.at[d], up_r.at[d], partner).wait_send()
                copy(pieces, pieces, down_s.at[d], down_r.at[d], partner).wait_send()
            totals = tz.at[d, 0 : nz - 1]
            copy(totals, totals, z_s.at[d], z_r.at[d, 0], partner).wait_send()
            for i in range(nz):

                @pl.when(z > i if flip else z < i)
                def _():
                    k = lax.rem(z - i + nz, nz)
                    total_from(k).wait_recv()

            if nx > 1:

                @pl.when(x != (0 if flip else nx - 1))
                def _():
                    chain_copy().wait_send()

        return drain

    forward_shift.wait_recv()
    start = jnp.where(first, states[...], shift_dst[0])
    c_buf[0] = jnp.where(first, 0.0, -coarse_of(start, False)) + relax(start)

    def extra_up():
        column_mats.pass_on()
        column_mats.finish()
        middle_y = (ny + 1) // 2
        pr[0] = eye
        sr[ny - 1] = eye

        def sooner(j):
            pr[j] = ry[0] if j == 1 else times(pr[j - 1], ry[j - 1])

        def later(j):
            sr[j] = ry[j + 1] if j == ny - 2 else times(ry[j + 1], sr[j + 1])

        for j in range(1, middle_y + 1):
            sooner(j)
        for j in range(ny - 2, middle_y - 2, -1):
            later(j)
        pz[z] = times(pr[middle_y], sr[middle_y - 1]) if ny > 1 else pr[1]
        z_mats.start()
        for j in range(middle_y + 1, ny):
            sooner(j)
        for j in range(middle_y - 2, -1, -1):
            later(j)

    forward_drain = scan(0, extra_up)
    results[0] = jnp.where(first, states[...], results[0])
    pltpu.make_async_copy(results.at[0], ns_out, out_sem.at[0]).start()

    def final_step(n, u):
        u_own[n] = u
        activ = activate(n, u)
        slopes[n] = 1.0 - activ * activ
        return u + STEP * activ

    lax.fori_loop(0, blocks, final_step, results[0])
    inputs_copy = copy(u_own, u_got, u_s, u_r, partner)
    inputs_copy.start()

    shift_src[1] = back_relax(guess[...])
    back_shift = copy(shift_src.at[1], shift_dst.at[1], shift_s.at[1], shift_r.at[1], behind)
    back_shift.start()
    new_ends = jnp.where(first, 0.0, coarse_of(results[0], False)) + c_buf[0]
    v_src[2] = new_ends
    pltpu.make_async_copy(v_src.at[2], ne_out, out_sem.at[0]).start()
    for n in range(blocks):
        xt[n] = beside(u_own[n])
    inputs_copy.wait_recv()
    for n in range(blocks):
        xt_got[n] = beside(u_got[n])
    z_mats.pass_on(late, near=False)
    back_shift.wait_recv()
    back_start = jnp.where(final, guess[...], shift_dst[1])
    c_buf[1] = jnp.where(final, 0.0, -coarse_of(back_start, True)) + back_relax(back_start)
    back_drain = scan(1, lambda: None)
    results[1] = jnp.where(final, guess[...], results[1])
    pltpu.make_async_copy(results.at[1], na_out, out_sem.at[0]).start()

    def sens_copy(n):
        return copy(sens_own.at[n], sens_got.at[n], sens_s, sens_r.at[n], partner)

    def bias_sum(sens):
        return jnp.sum(sens.astype(BF16).astype(F32), axis=0, keepdims=True)

    lam_ref[...] = results[1]
    for n in range(blocks - 1, -1, -1):
        sens = slopes[n] * lam_ref[...]
        sens_own[n] = sens
        sens_copy(n).start()
        place(sens)
        if n > 0:
            lam_ref[...] = lam_ref[...] + STEP * adjoint_conv(n)
        gb_sum[n : n + 1, :] = bias_sum(sens)
        g_own[n] = grad_product(xt[n])
    new_back = jnp.where(final, 0.0, coarse_of(results[1], True)) + c_buf[1]
    v_src[3] = new_back
    pltpu.make_async_copy(v_src.at[3], nb_out, out_sem.at[0]).start()
    factor = STEP / (nb * batch * cells)
    for n in range(blocks - 1, -1, -1):
        sens_copy(n).wait_recv()
        place(sens_got[n])
        gb_sum[n : n + 1, :] = factor * (gb_sum[n : n + 1, :] + bias_sum(sens_got[n]))
        total = factor * (g_own[n] + grad_product(xt_got[n]))
        for dy in range(3):
            for dx in range(3):
                g_sum[n, 3 * dy + dx] = total[ch * dx : ch * (dx + 1), ch * dy : ch * (dy + 1)]
        pltpu.make_async_copy(g_sum.at[n], gk_out.at[n], out_sem.at[1]).start()
    bias_out = pltpu.make_async_copy(gb_sum, gb_out, out_sem.at[2])
    bias_out.start()

    copy(sens_own, sens_got, sens_s, u_r, partner).wait_send()
    inputs_copy.wait_send()
    forward_shift.wait_send()
    back_shift.wait_send()
    row_mats.drain()
    column_mats.drain()
    z_mats.drain()
    for i in {0, nz - 1}:

        @pl.when(z != i)
        def _():
            z_mats.swap(i, lax.rem(z - i + nz, nz), other).wait_recv()

    forward_drain()
    back_drain()
    pltpu.make_async_copy(v_src, v_src, out_sem.at[0]).wait()
    pltpu.make_async_copy(g_sum, gk_out, out_sem.at[1]).wait()
    bias_out.wait()


def flush(*refs):
    sem = refs[-1]
    blocks = refs[4].shape[0]
    copies = [pltpu.make_async_copy(refs[4].at[n], refs[10].at[n], sem.at[n]) for n in range(blocks)]
    copies += [pltpu.make_async_copy(refs[i], refs[6 + i], sem.at[blocks + i]) for i in (0, 1, 2, 3, 5)]
    for c in copies:
        c.start()
    for c in copies:
        c.wait()


def body(sizes, kernels, biases, states, adjoint_guess):
    nz, ny, nx, nb = sizes
    plane = ny * nx
    blocks, taps, ch, _ = kernels.shape
    side = states.shape[2]
    batch = states.shape[1]
    cells = side * side
    own = cells // plane
    field = jax.ShapeDtypeStruct((cells, ch), F32)
    dma = pltpu.SemaphoreType.DMA
    vmem = pltpu.VMEM
    scratch = [
        vmem((blocks, taps * ch, ch), BF16),
        vmem((blocks, ch), F32),
        vmem((cells, ch), F32),
        vmem((cells, ch), F32),
        vmem((ch, ch), BF16),
        vmem((cells + 2 * side, ch), BF16),
        vmem((blocks, 3 * ch, cells), BF16),
        vmem((blocks, cells, ch), F32),
        vmem((nx, ch, ch), F32),
        vmem((ny, ch, ch), F32),
        vmem((nz, ch, ch), F32),
        vmem((nx + 1, ch, ch), F32),
        vmem((nx, ch, ch), F32),
        vmem((ny + 1, ch, ch), F32),
        vmem((ny, ch, ch), F32),
        vmem((2, cells, ch), F32),
        vmem((2, cells, ch), F32),
        vmem((2, cells, ch), F32),
        vmem((4, cells, ch), F32),
        vmem((2, cells, ch), F32),
        vmem((2, cells, ch), F32),
        vmem((2, plane, own, ch), F32),
        vmem((2, nz, own, ch), F32),
        vmem((own, ch), F32),
        vmem((2, ny, own, ch), F32),
        vmem((2, cells, ch), F32),
        vmem((2, cells, ch), F32),
        vmem((cells, ch), F32),
        vmem((blocks, cells, ch), F32),
        vmem((blocks, cells, ch), F32),
        vmem((blocks, 3 * ch, cells), BF16),
        vmem((blocks, cells, ch), F32),
        vmem((blocks, cells, ch), F32),
        vmem((blocks, 3 * ch, 3 * ch), F32),
        vmem((blocks, taps, ch, ch), F32),
        vmem((blocks, ch), F32),
        dma((5,)),
        dma((3,)),
        dma((6,)),
        dma((nx,)),
        dma((nx,)),
        dma((ny,)),
        dma((ny,)),
        dma((nz,)),
        dma((nz,)),
        dma((2,)),
        dma((2,)),
        dma((2,)),
        dma((2,)),
        dma((2,)),
        dma((2,)),
        dma((2,)),
        dma((2, nz)),
        dma((2,)),
        dma((2,)),
        dma(()),
        dma(()),
        dma(()),
        dma((blocks,)),
    ]
    any_space = pl.BlockSpec(memory_space=pl.ANY)
    outs = pl.pallas_call(
        functools.partial(kernel, sizes, blocks, side, batch),
        out_shape=[field] * 4
        + [jax.ShapeDtypeStruct((blocks, taps, ch, ch), F32), jax.ShapeDtypeStruct((blocks, ch), F32)],
        in_specs=[pl.BlockSpec(memory_space=pltpu.HBM)] * 4,
        out_specs=[any_space] * 6,
        scratch_shapes=scratch,
        compiler_params=pltpu.CompilerParams(
            collective_id=0, has_side_effects=True, vmem_limit_bytes=40 * 1024 * 1024
        ),
        name="vcycle",
    )(
        *(
            pltpu.with_memory_space_constraint(a, pltpu.HBM)
            for a in (
                kernels.reshape(blocks, taps * ch, ch),
                biases,
                states.reshape(cells, ch),
                adjoint_guess.reshape(cells, ch),
            )
        )
    )
    outs = pl.pallas_call(
        flush,
        out_shape=[jax.ShapeDtypeStruct(out.shape, out.dtype) for out in outs],
        in_specs=[any_space] * 6,
        out_specs=[pl.BlockSpec(memory_space=pltpu.HBM)] * 6,
        scratch_shapes=[dma((6 + blocks,))],
        compiler_params=pltpu.CompilerParams(vmem_limit_bytes=1024 * 1024),
        name="flush",
    )(*outs)
    fields = [out.reshape(states.shape) for out in outs[:4]]
    return (*fields, outs[4], outs[5])


def solution(mesh, sizes=(8, 4, 4)):
    sizes = (*sizes, mesh.shape["batch"])
    torus = Mesh(mesh.devices.reshape(sizes), AXES)
    state = P(LAYER, "batch", None, None, None)
    return jax.shard_map(
        functools.partial(body, sizes),
        mesh=torus,
        in_specs=(P(LAYER, None, None, None), P(LAYER, None), state, state),
        out_specs=(state, state, state, state, P(LAYER, None, None, None), P(LAYER, None)),
        check_vma=False,
    )
```

```python
import functools

import jax
import jax.numpy as jnp
from jax import lax
from jax.experimental import pallas as pl
from jax.experimental.pallas import tpu as pltpu
from jax.sharding import Mesh
from jax.sharding import PartitionSpec as P

LAYER = ("layer_0", "layer_1", "layer_2")
AXES = LAYER + ("batch",)
MESH = pl.DeviceIdType.MESH
STEP = 0.1
F32 = jnp.float32
BF16 = jnp.bfloat16


def split(value):
    high = value.astype(BF16)
    return high, (value - high.astype(F32)).astype(BF16)


def dot(left, right, flip=False):
    contract = (((1,), (1,)), ((), ())) if flip else (((1,), (0,)), ((), ()))
    return lax.dot_general(left, right, contract, preferred_element_type=F32)


def times_exact(left, exact, flip=False):
    high, low = split(left)
    return dot(high, exact, flip) + dot(low, exact, flip)


def exact_times(exact, right):
    high, low = split(right)
    return dot(exact, high) + dot(exact, low)


def times(left, right, flip=False):
    high, low = split(left)
    right_high, right_low = split(right)
    return dot(high, right_high, flip) + (dot(low, right_high, flip) + dot(high, right_low, flip))


def kernel(
    sizes, blocks, side,
    k_hbm, b_hbm, st_hbm, ad_hbm,
    ns_out, ne_out, na_out, nb_out, xt_out, sens_out,
    w, bias, states, guess, middle,
    xs, xt, slopes,
    kx, ry, pz, pm, sm, pr, sr,
    shift_src, shift_dst, c_buf, v_src, v_dst,
    w_src, up, tz, entering, row_src, down, results, lam_ref,
    u_all, sens_all,
    in_sem, out_sem,
    mat_s, x_r, xp_r, y_r, yp_r, zm_r, zp_r,
    shift_s, shift_r, chain_s, chain_r,
    up_s, up_r, z_s, z_r, down_s, down_r,
    u_s, u_r, sens_s, sens_r,
):
    nz, ny, nx, nb = sizes
    plane = ny * nx
    ch = w.shape[-1]
    cells = side * side
    own_cells = cells // plane
    coarse_step = blocks * STEP
    z, y, x = (lax.axis_index(a) for a in LAYER)
    b = lax.axis_index("batch")
    me = y * nx + x
    pos = z * plane + me
    last = nz * plane - 1
    first = pos == 0
    final = pos == last

    def device(position):
        return (position // plane, lax.rem(position // nx, ny), lax.rem(position, nx), b)

    ahead = device(lax.rem(pos + 1, last + 1))
    behind = device(lax.rem(pos + last, last + 1))
    partner = (z, y, x, 1 - b)

    def ring(step, size):
        return min(step, size - step)

    offsets = sorted(
        ((dy, dx) for dy in range(ny) for dx in range(nx) if dy or dx),
        key=lambda o: -ring(o[0], ny) - ring(o[1], nx),
    )
    z_steps = sorted(range(1, nz), key=lambda k: -ring(k, nz))

    def mate(offset):
        ty, tx = lax.rem(y + offset[0], ny), lax.rem(x + offset[1], nx)
        return ty, ty * nx + tx, (z, ty, tx, b)

    def copy(src, dst, send, recv, to):
        return pltpu.make_async_remote_copy(
            src_ref=src, dst_ref=dst, send_sem=send, recv_sem=recv, device_id=to, device_id_type=MESH
        )

    loads = [
        pltpu.make_async_copy(k_hbm.at[0, 4 * ch : 5 * ch], middle, in_sem.at[0]),
        pltpu.make_async_copy(st_hbm, states, in_sem.at[1]),
        pltpu.make_async_copy(b_hbm, bias, in_sem.at[2]),
        pltpu.make_async_copy(k_hbm, w, in_sem.at[3]),
        pltpu.make_async_copy(ad_hbm, guess, in_sem.at[4]),
    ]
    for c in loads:
        c.start()

    barrier = pltpu.get_barrier_semaphore()

    def greet(to):
        pl.semaphore_signal(barrier, inc=1, device_id=to, device_id_type=MESH)

    greet(ahead)
    greet(behind)
    greet(partner)
    for o in offsets:
        greet(mate(o)[2])
    for k in range(1, nz):
        greet((lax.rem(z + k, nz), y, x, b))
    greeted = 3 + plane - 1 + nz - 1

    xs[0:side, :] = jnp.zeros((side, ch), BF16)
    xs[side + cells : 2 * side + cells, :] = jnp.zeros((side, ch), BF16)

    @pl.when(first)
    def _():
        shift_dst[0] = jnp.zeros((cells, ch), F32)

    @pl.when(final)
    def _():
        shift_dst[1] = jnp.zeros((cells, ch), F32)

    column = lax.rem(lax.broadcasted_iota(jnp.int32, (cells, ch), 0), side)
    inner_left = column != 0
    inner_right = column != side - 1

    def place(value):
        xs[side : side + cells, :] = value.astype(BF16)

    def rows_beside():
        return [xs[side * dy : side * dy + cells, :] for dy in range(3)]

    def from_left(value):
        return jnp.where(inner_left, pltpu.roll(value, 1, 0), 0.0)

    def from_right(value):
        return jnp.where(inner_right, pltpu.roll(value, cells - 1, 0), 0.0)

    def join_columns(wide):
        return wide[:, ch : 2 * ch] + (from_left(wide[:, :ch]) + from_right(wide[:, 2 * ch :]))

    def tap(n, t):
        return w[n, ch * t : ch * (t + 1), :]

    def activate(n, u):
        place(u)
        weights = jnp.concatenate(
            [jnp.concatenate([tap(n, 3 * dy + dx) for dx in range(3)], axis=1) for dy in range(3)], axis=0
        )
        wide = dot(jnp.concatenate(rows_beside(), axis=1), weights)
        return jnp.tanh(join_columns(wide) + bias[pl.ds(n, 1), :])

    def adjoint_conv(n):
        flipped = jnp.concatenate(
            [jnp.concatenate([tap(n, 8 - 3 * dy - dx) for dy in range(3)], axis=1) for dx in range(3)], axis=0
        )
        return join_columns(dot(jnp.concatenate(rows_beside(), axis=1), flipped, True))

    def beside(u):
        return jnp.concatenate([jnp.transpose(v).astype(BF16) for v in (from_left(u), u, from_right(u))], axis=0)

    def relax(u):
        return lax.fori_loop(0, blocks, lambda n, s: s + STEP * activate(n, s), u, unroll=True)

    def back_relax(lam):
        def body(k, lam):
            n = blocks - 1 - k
            place(slopes[n] * lam)
            return lam + STEP * adjoint_conv(n)

        return lax.fori_loop(0, blocks, body, lam, unroll=True)

    eye = (
        lax.broadcasted_iota(jnp.int32, (ch, ch), 0) == lax.broadcasted_iota(jnp.int32, (ch, ch), 1)
    ).astype(F32)
    half = ch // nb
    mine = pl.ds(pl.multiple_of(half * b, half), half)
    other = pl.ds(pl.multiple_of(half * (1 - b), half), half)

    class Maps:
        def __init__(self, buf, index, size, to, send, recv, pair_send, pair_recv):
            self.buf, self.index, self.size, self.to = buf, index, size, to
            self.send, self.recv, self.pair_send, self.pair_recv = send, recv, pair_send, pair_recv
            near = [k for k in range(1, size) if ring(k, size) <= 2]
            near.sort(key=lambda k: -ring(k, size))
            far = [k for k in range(size - 1, 0, -1) if ring(k, size) > 2]
            self.near, self.far = near, far

        def source(self, k):
            return lax.rem(self.index - k + self.size, self.size)

        def move(self, source, k, target):
            part = self.buf.at[source, mine]
            return copy(part, part, self.send, self.recv.at[k], target)

        def swap(self, source, k, rows):
            part = self.buf.at[source, rows]
            return copy(part, part, self.pair_send, self.pair_recv.at[k], partner)

        def start(self):
            for k in self.near:
                self.move(self.index, k, self.to(lax.rem(self.index + k, self.size))).start()

        def pass_on(self, wanted=None, near=True, far=True):
            for k in (self.near if near else []) + (self.far if far else []):
                source = self.source(k)

                def take(k=k, source=source):
                    self.move(source, k, partner).wait_recv()
                    for f in self.far:
                        if k == (2 if f <= self.size // 2 else self.size - 2):
                            self.move(source, f, self.to(lax.rem(self.index + f - k + self.size, self.size))).start()
                    self.swap(source, k, mine).start()

                if wanted is None:
                    take()
                else:
                    pl.when(wanted(k, source))(take)

        def finish(self):
            for k in range(1, self.size):
                self.swap(self.source(k), k, other).wait_recv()

        def drain(self):
            if self.size > 1:
                part = self.buf.at[0 : self.size - 1, mine]
                copy(part, part, self.send, self.recv.at[0], partner).wait_send()
                copy(part, part, self.pair_send, self.recv.at[0], partner).wait_send()

    row_mats = Maps(kx, x, nx, lambda t: (z, y, t, b), mat_s.at[0], x_r, mat_s.at[1], xp_r)
    column_mats = Maps(ry, y, ny, lambda t: (z, t, x, b), mat_s.at[2], y_r, mat_s.at[3], yp_r)
    z_mats = Maps(pz, z, nz, lambda t: (t, y, x, b), mat_s.at[4], zm_r, mat_s.at[5], zp_r)

    for c in loads:
        c.wait()
    kx[x] = middle[...].astype(F32)
    relaxed = relax(states[...])
    pl.semaphore_wait(barrier, greeted)
    row_mats.start()
    shift_src[0] = relaxed
    forward_shift = copy(shift_src.at[0], shift_dst.at[0], shift_s.at[0], shift_r.at[0], ahead)
    pl.when(pos != last)(forward_shift.start)

    row_mats.pass_on()
    row_mats.finish()
    def step_map(j):
        return eye + coarse_step * kx[j]

    middle_x = (nx + 1) // 2
    pm[0] = eye
    sm[nx - 1] = eye

    def row_sooner_map(j):
        pm[j] = step_map(0) if j == 1 else pm[j - 1] + coarse_step * times_exact(pm[j - 1], kx[j - 1].astype(BF16))

    def row_later_map(j):
        first_later = step_map(j + 1)
        sm[j] = first_later if j == nx - 2 else sm[j + 1] + coarse_step * exact_times(kx[j + 1].astype(BF16), sm[j + 1])

    for j in range(1, middle_x + 1):
        row_sooner_map(j)
    for j in range(nx - 2, middle_x - 2, -1):
        row_later_map(j)
    ry[y] = times(pm[middle_x], sm[middle_x - 1]) if nx > 1 else pm[1]
    column_mats.start()
    for j in range(middle_x + 1, nx):
        row_sooner_map(j)
    for j in range(middle_x - 2, -1, -1):
        row_later_map(j)

    def early(k, source):
        needed = (source < z) & (source != 0)
        return needed | (z == 0) if k == nz - 2 and nz > 4 else needed

    def late(k, source):
        return jnp.logical_not(early(k, source))

    def coarse_of(field, flip):
        return field + coarse_step * times_exact(field, middle[...], flip)

    def scan(d, extra_up):
        flip = d == 1
        row_later, row_sooner = (pm, sm) if flip else (sm, pm)
        column_later, column_sooner = (pr, sr) if flip else (sr, pr)
        w_src[d] = times(c_buf[d], row_later[x], flip)
        for o in offsets:
            _, t, to = mate(o)
            piece = pl.ds(pl.multiple_of(own_cells * t, own_cells), own_cells)
            copy(w_src.at[d, piece], up.at[d, me], up_s.at[d], up_r.at[d], to).start()
        own = pl.ds(pl.multiple_of(own_cells * me, own_cells), own_cells)
        up[d, me] = w_src[d, own]

        def chain_copy():
            to = lax.rem(x + (nx - 1 if flip else 1), nx)
            return copy(v_src.at[d], v_dst.at[d], chain_s.at[d], chain_r.at[d], (z, y, to, b))

        def chain(k):
            sender = nx - 1 - k if flip else k
            if k >= nx - 1:
                return

            @pl.when(x == sender)
            def _():
                if k == 0:
                    v_src[d] = c_buf[d]
                else:
                    chain_copy().wait_recv()
                    v_src[d] = coarse_of(v_dst[d], flip) + c_buf[d]
                chain_copy().start()

        extra_up()
        chain(0)
        pieces = up.at[d, 0 : plane - 1]
        if plane > 1:
            copy(pieces, pieces, up_s.at[d], up_r.at[d], partner).wait_recv()
        row_total = [sum(up[d, r * nx + i] for i in range(nx)) for r in range(ny)]
        tz[d, z] = sum(times(row_total[r], column_later[r], flip) for r in range(ny))
        for k in z_steps:
            to = lax.rem(z + k, nz)
            copy(tz.at[d, z], tz.at[d, z], z_s.at[d], z_r.at[d, k], (to, y, x, b)).start()
        inside = [None] * ny
        order = list(range(ny - 1, -1, -1)) if flip else list(range(ny))
        inside[order[0]] = jnp.zeros((own_cells, ch), F32)
        for r, s in zip(order, order[1:]):
            inside[s] = times(inside[r], ry[r], flip) + row_total[r]
        if not flip:
            z_mats.pass_on(early)
        chain(1)

        def total_from(k):
            source = lax.rem(z - k + nz, nz)
            return copy(tz.at[d, source], tz.at[d, source], z_s.at[d], z_r.at[d, k], partner)

        entering[...] = jnp.zeros((own_cells, ch), F32)
        for i in range(nz - 1, 0, -1) if flip else range(nz - 1):

            @pl.when(z < i if flip else z > i)
            def _():
                k = lax.rem(z - i + nz, nz)
                total_from(k).wait_recv()
                if i == (nz - 1 if flip else 0):
                    entering[...] = tz[d, i]
                else:
                    z_mats.swap(i, k, other).wait_recv()
                    entering[...] = times(entering[...], pz[i], flip) + tz[d, i]

        for r in range(ny):
            row_src[d, r] = times(entering[...], column_sooner[r], flip) + inside[r]
        for o in offsets:
            ty, _, to = mate(o)
            copy(row_src.at[d, ty], down.at[d, own], down_s.at[d], down_r.at[d], to).start()
        down[d, own] = row_src[d, y]
        for k in range(2, nx - 1):
            chain(k)
        if not flip:
            z_mats.pass_on(late, far=False)
        if plane > 1:
            copy(pieces, pieces, down_s.at[d], down_r.at[d], partner).wait_recv()
        results[d] = times(down[d], row_sooner[x], flip)

        if nx > 1:

            @pl.when(x == (0 if flip else nx - 1))
            def _():
                chain_copy().wait_recv()

            @pl.when(x != (nx - 1 if flip else 0))
            def _():
                results[d] = results[d] + v_dst[d]

        def drain():
            if plane > 1:
                copy(pieces, pieces, up_s.at[d], up_r.at[d], partner).wait_send()
                copy(pieces, pieces, down_s.at[d], down_r.at[d], partner).wait_send()
            totals = tz.at[d, 0 : nz - 1]
            copy(totals, totals, z_s.at[d], z_r.at[d, 0], partner).wait_send()
            for i in range(nz):

                @pl.when(z > i if flip else z < i)
                def _():
                    k = lax.rem(z - i + nz, nz)
                    total_from(k).wait_recv()

            if nx > 1:

                @pl.when(x != (0 if flip else nx - 1))
                def _():
                    chain_copy().wait_send()

        return drain

    pl.when(pos != 0)(forward_shift.wait_recv)
    start = jnp.where(first, states[...], shift_dst[0])
    c_buf[0] = jnp.where(first, 0.0, -coarse_of(start, False)) + relax(start)

    def extra_up():
        column_mats.pass_on()
        column_mats.finish()
        middle_y = (ny + 1) // 2
        pr[0] = eye
        sr[ny - 1] = eye

        def sooner(j):
            pr[j] = ry[0] if j == 1 else times(pr[j - 1], ry[j - 1])

        def later(j):
            sr[j] = ry[j + 1] if j == ny - 2 else times(ry[j + 1], sr[j + 1])

        for j in range(1, middle_y + 1):
            sooner(j)
        for j in range(ny - 2, middle_y - 2, -1):
            later(j)
        pz[z] = times(pr[middle_y], sr[middle_y - 1]) if ny > 1 else pr[1]
        z_mats.start()
        for j in range(middle_y + 1, ny):
            sooner(j)
        for j in range(middle_y - 2, -1, -1):
            later(j)

    forward_drain = scan(0, extra_up)
    results[0] = jnp.where(first, states[...], results[0])
    pltpu.make_async_copy(results.at[0], ns_out, out_sem.at[0]).start()

    def final_step(n, u):
        u_all[b, n] = u
        activ = activate(n, u)
        slopes[n] = 1.0 - activ * activ
        return u + STEP * activ

    lax.fori_loop(0, blocks, final_step, results[0], unroll=True)
    inputs_copy = copy(u_all.at[b], u_all.at[b], u_s, u_r, partner)
    inputs_copy.start()

    shift_src[1] = back_relax(guess[...])
    back_shift = copy(shift_src.at[1], shift_dst.at[1], shift_s.at[1], shift_r.at[1], behind)
    pl.when(pos != 0)(back_shift.start)
    new_ends = jnp.where(first, 0.0, coarse_of(results[0], False)) + c_buf[0]
    v_src[2] = new_ends
    pltpu.make_async_copy(v_src.at[2], ne_out, out_sem.at[0]).start()
    inputs_copy.wait_recv()
    for n in range(blocks):
        for i in range(nb):
            xt[n, :, cells * i : cells * (i + 1)] = beside(u_all[i, n])
    inputs_out = pltpu.make_async_copy(xt, xt_out, out_sem.at[1])
    inputs_out.start()
    z_mats.pass_on(late, near=False)
    pl.when(pos != last)(back_shift.wait_recv)
    back_start = jnp.where(final, guess[...], shift_dst[1])
    c_buf[1] = jnp.where(final, 0.0, -coarse_of(back_start, True)) + back_relax(back_start)
    back_drain = scan(1, lambda: None)
    results[1] = jnp.where(final, guess[...], results[1])
    pltpu.make_async_copy(results.at[1], na_out, out_sem.at[0]).start()

    def sens_copy(n):
        return copy(sens_all.at[n, b], sens_all.at[n, b], sens_s, sens_r.at[n], partner)

    lam_ref[...] = results[1]
    for n in range(blocks - 1, -1, -1):
        sens = slopes[n] * lam_ref[...]
        sens_all[n, b] = sens
        sens_copy(n).start()
        if n > 0:
            place(sens)
            lam_ref[...] = lam_ref[...] + STEP * adjoint_conv(n)
    new_back = jnp.where(final, 0.0, coarse_of(results[1], True)) + c_buf[1]
    v_src[3] = new_back
    pltpu.make_async_copy(v_src.at[3], nb_out, out_sem.at[0]).start()
    for n in range(blocks - 1, -1, -1):
        got = sens_all.at[n, 1 - b]
        copy(got, got, sens_s, sens_r.at[n], partner).wait_recv()
        pltpu.make_async_copy(sens_all.at[n], sens_out.at[n], out_sem.at[2]).start()

    copy(u_all.at[0], u_all.at[0], sens_s, u_r, partner).wait_send()
    inputs_copy.wait_send()
    pl.when(pos != last)(forward_shift.wait_send)
    pl.when(pos != 0)(back_shift.wait_send)
    row_mats.drain()
    column_mats.drain()
    z_mats.drain()
    for i in {0, nz - 1}:

        @pl.when(z != i)
        def _():
            z_mats.swap(i, lax.rem(z - i + nz, nz), other).wait_recv()

    forward_drain()
    back_drain()
    pltpu.make_async_copy(v_src, v_src, out_sem.at[0]).wait()
    inputs_out.wait()
    pltpu.make_async_copy(sens_all, sens_out, out_sem.at[2]).wait()


def gradients(
    factor, side,
    ns, ne, na, nb, xt, sens,
    ns_out, ne_out, na_out, nb_out, gk_out, gb_out,
    xs, grads, bias_grads, out_sem,
):
    blocks, images, cells, ch = sens.shape
    outs = [
        pltpu.make_async_copy(a, out, out_sem.at[blocks + 1 + i])
        for i, (a, out) in enumerate(((ns, ns_out), (ne, ne_out), (na, na_out), (nb, nb_out)))
    ]
    for c in outs:
        c.start()
    for i in range(images):
        xs[i, 0:side, :] = jnp.zeros((side, ch), BF16)
        xs[i, side + cells : 2 * side + cells, :] = jnp.zeros((side, ch), BF16)
    for n in range(blocks):
        bias_sum = jnp.zeros((1, ch), F32)
        for i in range(images):
            rounded = sens[n, i].astype(BF16)
            xs[i, side : side + cells, :] = rounded
            bias_sum = bias_sum + jnp.sum(rounded.astype(F32), axis=0, keepdims=True)
        bias_grads[n : n + 1, :] = factor * bias_sum
        rows = [
            jnp.concatenate([xs[i, side * dy : side * dy + cells, :] for dy in (2, 1, 0)], axis=1)
            for i in range(images)
        ]
        total = factor * dot(xt[n], jnp.concatenate(rows, axis=0))
        for dy in range(3):
            for dx in range(3):
                grads[n, 3 * dy + dx] = total[ch * dx : ch * (dx + 1), ch * dy : ch * (dy + 1)]
        outs.append(pltpu.make_async_copy(grads.at[n], gk_out.at[n], out_sem.at[n]))
        outs[-1].start()
    outs.append(pltpu.make_async_copy(bias_grads, gb_out, out_sem.at[blocks]))
    outs[-1].start()
    for c in outs:
        c.wait()


def body(sizes, kernels, biases, states, adjoint_guess):
    nz, ny, nx, nb = sizes
    plane = ny * nx
    blocks, taps, ch, _ = kernels.shape
    side = states.shape[2]
    batch = states.shape[1]
    cells = side * side
    own = cells // plane
    field = jax.ShapeDtypeStruct((cells, ch), F32)
    dma = pltpu.SemaphoreType.DMA
    vmem = pltpu.VMEM
    scratch = [
        vmem((blocks, taps * ch, ch), BF16),
        vmem((blocks, ch), F32),
        vmem((cells, ch), F32),
        vmem((cells, ch), F32),
        vmem((ch, ch), BF16),
        vmem((cells + 2 * side, ch), BF16),
        vmem((blocks, 3 * ch, nb * cells), BF16),
        vmem((blocks, cells, ch), F32),
        vmem((nx, ch, ch), F32),
        vmem((ny, ch, ch), F32),
        vmem((nz, ch, ch), F32),
        vmem((nx + 1, ch, ch), F32),
        vmem((nx, ch, ch), F32),
        vmem((ny + 1, ch, ch), F32),
        vmem((ny, ch, ch), F32),
        vmem((2, cells, ch), F32),
        vmem((2, cells, ch), F32),
        vmem((2, cells, ch), F32),
        vmem((4, cells, ch), F32),
        vmem((2, cells, ch), F32),
        vmem((2, cells, ch), F32),
        vmem((2, plane, own, ch), F32),
        vmem((2, nz, own, ch), F32),
        vmem((own, ch), F32),
        vmem((2, ny, own, ch), F32),
        vmem((2, cells, ch), F32),
        vmem((2, cells, ch), F32),
        vmem((cells, ch), F32),
        vmem((nb, blocks, cells, ch), F32),
        vmem((blocks, nb, cells, ch), F32),
        dma((5,)),
        dma((3,)),
        dma((6,)),
        dma((nx,)),
        dma((nx,)),
        dma((ny,)),
        dma((ny,)),
        dma((nz,)),
        dma((nz,)),
        dma((2,)),
        dma((2,)),
        dma((2,)),
        dma((2,)),
        dma((2,)),
        dma((2,)),
        dma((2,)),
        dma((2, nz)),
        dma((2,)),
        dma((2,)),
        dma(()),
        dma(()),
        dma(()),
        dma((blocks,)),
    ]
    any_space = pl.BlockSpec(memory_space=pl.ANY)
    outs = pl.pallas_call(
        functools.partial(kernel, sizes, blocks, side),
        out_shape=[field] * 4
        + [
            jax.ShapeDtypeStruct((blocks, 3 * ch, nb * cells), BF16),
            jax.ShapeDtypeStruct((blocks, nb, cells, ch), F32),
        ],
        in_specs=[pl.BlockSpec(memory_space=pltpu.HBM)] * 4,
        out_specs=[any_space] * 6,
        scratch_shapes=scratch,
        compiler_params=pltpu.CompilerParams(
            collective_id=0, has_side_effects=True, vmem_limit_bytes=40 * 1024 * 1024
        ),
        name="vcycle",
    )(
        *(
            pltpu.with_memory_space_constraint(a, pltpu.HBM)
            for a in (
                kernels.reshape(blocks, taps * ch, ch),
                biases,
                states.reshape(cells, ch),
                adjoint_guess.reshape(cells, ch),
            )
        )
    )
    outs = pl.pallas_call(
        functools.partial(gradients, STEP / (nb * batch * cells), side),
        out_shape=[field] * 4
        + [jax.ShapeDtypeStruct((blocks, taps, ch, ch), F32), jax.ShapeDtypeStruct((blocks, ch), F32)],
        in_specs=[any_space] * 4 + [pl.BlockSpec(memory_space=vmem)] * 2,
        out_specs=[pl.BlockSpec(memory_space=pltpu.HBM)] * 6,
        scratch_shapes=[
            vmem((nb, cells + 2 * side, ch), BF16),
            vmem((blocks, taps, ch, ch), F32),
            vmem((blocks, ch), F32),
            dma((blocks + 5,)),
        ],
        compiler_params=pltpu.CompilerParams(vmem_limit_bytes=16 * 1024 * 1024),
        name="gradients",
    )(*outs)
    fields = [out.reshape(states.shape) for out in outs[:4]]
    return (*fields, outs[4], outs[5])


def solution(mesh, sizes=(8, 4, 4)):
    sizes = (*sizes, mesh.shape["batch"])
    torus = Mesh(mesh.devices.reshape(sizes), AXES)
    state = P(LAYER, "batch", None, None, None)
    return jax.shard_map(
        functools.partial(body, sizes),
        mesh=torus,
        in_specs=(P(LAYER, None, None, None), P(LAYER, None), state, state),
        out_specs=(state, state, state, state, P(LAYER, None, None, None), P(LAYER, None)),
        check_vma=False,
    )
```

```python
import functools

import jax
import jax.numpy as jnp
from jax import lax
from jax.experimental import pallas as pl
from jax.experimental.pallas import tpu as pltpu
from jax.sharding import Mesh
from jax.sharding import PartitionSpec as P

LAYER = ("layer_0", "layer_1", "layer_2")
AXES = LAYER + ("batch",)
MESH = pl.DeviceIdType.MESH
STEP = 0.1
F32 = jnp.float32
BF16 = jnp.bfloat16


def split(value):
    high = value.astype(BF16)
    return high, (value - high.astype(F32)).astype(BF16)


def dot(left, right, flip=False):
    contract = (((1,), (1,)), ((), ())) if flip else (((1,), (0,)), ((), ()))
    return lax.dot_general(left, right, contract, preferred_element_type=F32)


def times_exact(left, exact, flip=False):
    high, low = split(left)
    return dot(high, exact, flip) + dot(low, exact, flip)


def exact_times(exact, right):
    high, low = split(right)
    return dot(exact, high) + dot(exact, low)


def times(left, right, flip=False):
    high, low = split(left)
    right_high, right_low = split(right)
    return dot(high, right_high, flip) + (dot(low, right_high, flip) + dot(high, right_low, flip))


def kernel(
    sizes, blocks, side,
    k_hbm, b_hbm, st_hbm, ad_hbm,
    ns_out, ne_out, na_out, nb_out, xt_out, sens_out,
    w, bias, states, guess, middle,
    xs, xt, slopes,
    kx, ry, pz, pm, sm, pr, sr,
    shift_src, shift_dst, c_buf, v_src, v_dst,
    w_src, up, tz, entering, row_src, down, results, lam_ref,
    u_all, sens_all,
    in_sem, out_sem,
    mat_s, x_r, xp_r, y_r, yp_r, zm_r, zp_r,
    shift_s, shift_r, chain_s, chain_r,
    up_s, up_r, z_s, z_r, down_s, down_r,
    u_s, u_r, sens_s, sens_r,
):
    nz, ny, nx, nb = sizes
    plane = ny * nx
    ch = w.shape[-1]
    cells = side * side
    own_cells = cells // plane
    coarse_step = blocks * STEP
    z, y, x = (lax.axis_index(a) for a in LAYER)
    b = lax.axis_index("batch")
    me = y * nx + x
    pos = z * plane + me
    last = nz * plane - 1
    first = pos == 0
    final = pos == last

    def device(position):
        return (position // plane, lax.rem(position // nx, ny), lax.rem(position, nx), b)

    ahead = device(lax.rem(pos + 1, last + 1))
    behind = device(lax.rem(pos + last, last + 1))
    partner = (z, y, x, 1 - b)

    def ring(step, size):
        return min(step, size - step)

    offsets = sorted(
        ((dy, dx) for dy in range(ny) for dx in range(nx) if dy or dx),
        key=lambda o: -ring(o[0], ny) - ring(o[1], nx),
    )
    z_steps = sorted(range(1, nz), key=lambda k: -ring(k, nz))

    def mate(offset):
        ty, tx = lax.rem(y + offset[0], ny), lax.rem(x + offset[1], nx)
        return ty, ty * nx + tx, (z, ty, tx, b)

    def copy(src, dst, send, recv, to):
        return pltpu.make_async_remote_copy(
            src_ref=src, dst_ref=dst, send_sem=send, recv_sem=recv, device_id=to, device_id_type=MESH
        )

    weight_loads = [pltpu.make_async_copy(k_hbm.at[n], w.at[n], in_sem.at[4 + n]) for n in range(blocks)]
    first_loads = [
        pltpu.make_async_copy(st_hbm, states, in_sem.at[0]),
        pltpu.make_async_copy(b_hbm, bias, in_sem.at[1]),
    ]
    later_loads = [
        pltpu.make_async_copy(k_hbm.at[0, 4 * ch : 5 * ch], middle, in_sem.at[2]),
        pltpu.make_async_copy(ad_hbm, guess, in_sem.at[3]),
    ]
    for c in (weight_loads[0], *first_loads, *weight_loads[1:], *later_loads):
        c.start()

    barrier = pltpu.get_barrier_semaphore()

    def greet(to):
        pl.semaphore_signal(barrier, inc=1, device_id=to, device_id_type=MESH)

    greet(ahead)
    greet(behind)
    greet(partner)
    for o in offsets:
        greet(mate(o)[2])
    for k in range(1, nz):
        greet((lax.rem(z + k, nz), y, x, b))
    greeted = 3 + plane - 1 + nz - 1

    xs[0:side, :] = jnp.zeros((side, ch), BF16)
    xs[side + cells : 2 * side + cells, :] = jnp.zeros((side, ch), BF16)

    @pl.when(first)
    def _():
        shift_dst[0] = jnp.zeros((cells, ch), F32)

    @pl.when(final)
    def _():
        shift_dst[1] = jnp.zeros((cells, ch), F32)

    column = lax.rem(lax.broadcasted_iota(jnp.int32, (cells, ch), 0), side)
    inner_left = column != 0
    inner_right = column != side - 1

    def place(value):
        xs[side : side + cells, :] = value.astype(BF16)

    def rows_beside():
        return [xs[side * dy : side * dy + cells, :] for dy in range(3)]

    def from_left(value):
        return jnp.where(inner_left, pltpu.roll(value, 1, 0), 0.0)

    def from_right(value):
        return jnp.where(inner_right, pltpu.roll(value, cells - 1, 0), 0.0)

    def join_columns(wide):
        return wide[:, ch : 2 * ch] + (from_left(wide[:, :ch]) + from_right(wide[:, 2 * ch :]))

    def tap(n, t):
        return w[n, ch * t : ch * (t + 1), :]

    def activate(n, u):
        place(u)
        weights = jnp.concatenate(
            [jnp.concatenate([tap(n, 3 * dy + dx) for dx in range(3)], axis=1) for dy in range(3)], axis=0
        )
        wide = dot(jnp.concatenate(rows_beside(), axis=1), weights)
        return jnp.tanh(join_columns(wide) + bias[pl.ds(n, 1), :])

    def adjoint_conv(n):
        flipped = jnp.concatenate(
            [jnp.concatenate([tap(n, 8 - 3 * dy - dx) for dy in range(3)], axis=1) for dx in range(3)], axis=0
        )
        return join_columns(dot(jnp.concatenate(rows_beside(), axis=1), flipped, True))

    def beside(u):
        return jnp.concatenate([jnp.transpose(v).astype(BF16) for v in (from_left(u), u, from_right(u))], axis=0)

    def relax(u):
        return lax.fori_loop(0, blocks, lambda n, s: s + STEP * activate(n, s), u, unroll=True)

    def back_relax(lam):
        def body(k, lam):
            n = blocks - 1 - k
            place(slopes[n] * lam)
            return lam + STEP * adjoint_conv(n)

        return lax.fori_loop(0, blocks, body, lam, unroll=True)

    eye = (
        lax.broadcasted_iota(jnp.int32, (ch, ch), 0) == lax.broadcasted_iota(jnp.int32, (ch, ch), 1)
    ).astype(F32)
    half = ch // nb
    mine = pl.ds(pl.multiple_of(half * b, half), half)
    other = pl.ds(pl.multiple_of(half * (1 - b), half), half)

    class Maps:
        def __init__(self, buf, index, size, to, send, recv, pair_send, pair_recv):
            self.buf, self.index, self.size, self.to = buf, index, size, to
            self.send, self.recv, self.pair_send, self.pair_recv = send, recv, pair_send, pair_recv
            near = [k for k in range(1, size) if ring(k, size) <= 2]
            near.sort(key=lambda k: -ring(k, size))
            far = [k for k in range(size - 1, 0, -1) if ring(k, size) > 2]
            self.near, self.far = near, far

        def source(self, k):
            return lax.rem(self.index - k + self.size, self.size)

        def move(self, source, k, target):
            part = self.buf.at[source, mine]
            return copy(part, part, self.send, self.recv.at[k], target)

        def swap(self, source, k, rows):
            part = self.buf.at[source, rows]
            return copy(part, part, self.pair_send, self.pair_recv.at[k], partner)

        def start(self):
            for k in self.near:
                self.move(self.index, k, self.to(lax.rem(self.index + k, self.size))).start()

        def pass_on(self, wanted=None, near=True, far=True):
            for k in (self.near if near else []) + (self.far if far else []):
                source = self.source(k)

                def take(k=k, source=source):
                    self.move(source, k, partner).wait_recv()
                    for f in self.far:
                        if k == (2 if f <= self.size // 2 else self.size - 2):
                            self.move(source, f, self.to(lax.rem(self.index + f - k + self.size, self.size))).start()
                    self.swap(source, k, mine).start()

                if wanted is None:
                    take()
                else:
                    pl.when(wanted(k, source))(take)

        def finish(self):
            for k in range(1, self.size):
                self.swap(self.source(k), k, other).wait_recv()

        def drain(self):
            if self.size > 1:
                part = self.buf.at[0 : self.size - 1, mine]
                copy(part, part, self.send, self.recv.at[0], partner).wait_send()
                copy(part, part, self.pair_send, self.recv.at[0], partner).wait_send()

    row_mats = Maps(kx, x, nx, lambda t: (z, y, t, b), mat_s.at[0], x_r, mat_s.at[1], xp_r)
    column_mats = Maps(ry, y, ny, lambda t: (z, t, x, b), mat_s.at[2], y_r, mat_s.at[3], yp_r)
    z_mats = Maps(pz, z, nz, lambda t: (t, y, x, b), mat_s.at[4], zm_r, mat_s.at[5], zp_r)

    for c in first_loads:
        c.wait()
    relaxed = states[...]
    for n in range(blocks):
        weight_loads[n].wait()
        relaxed = relaxed + STEP * activate(n, relaxed)
    for c in later_loads:
        c.wait()
    kx[x] = middle[...].astype(F32)
    pl.semaphore_wait(barrier, greeted)
    row_mats.start()
    shift_src[0] = relaxed
    forward_shift = copy(shift_src.at[0], shift_dst.at[0], shift_s.at[0], shift_r.at[0], ahead)
    pl.when(pos != last)(forward_shift.start)

    row_mats.pass_on()
    row_mats.finish()
    def step_map(j):
        return eye + coarse_step * kx[j]

    middle_x = (nx + 1) // 2
    pm[0] = eye
    sm[nx - 1] = eye

    def row_sooner_map(j):
        pm[j] = step_map(0) if j == 1 else pm[j - 1] + coarse_step * times_exact(pm[j - 1], kx[j - 1].astype(BF16))

    def row_later_map(j):
        first_later = step_map(j + 1)
        sm[j] = first_later if j == nx - 2 else sm[j + 1] + coarse_step * exact_times(kx[j + 1].astype(BF16), sm[j + 1])

    for j in range(1, middle_x + 1):
        row_sooner_map(j)
    for j in range(nx - 2, middle_x - 2, -1):
        row_later_map(j)
    ry[y] = times(pm[middle_x], sm[middle_x - 1]) if nx > 1 else pm[1]
    column_mats.start()
    for j in range(middle_x + 1, nx):
        row_sooner_map(j)
    for j in range(middle_x - 2, -1, -1):
        row_later_map(j)

    def early(k, source):
        needed = (source < z) & (source != 0)
        return needed | (z == 0) if k == nz - 2 and nz > 4 else needed

    def late(k, source):
        return jnp.logical_not(early(k, source))

    def coarse_of(field, flip):
        return field + coarse_step * times_exact(field, middle[...], flip)

    def scan(d, extra_up):
        flip = d == 1
        row_later, row_sooner = (pm, sm) if flip else (sm, pm)
        column_later, column_sooner = (pr, sr) if flip else (sr, pr)
        w_src[d] = times(c_buf[d], row_later[x], flip)
        for o in offsets:
            _, t, to = mate(o)
            piece = pl.ds(pl.multiple_of(own_cells * t, own_cells), own_cells)
            copy(w_src.at[d, piece], up.at[d, me], up_s.at[d], up_r.at[d], to).start()
        own = pl.ds(pl.multiple_of(own_cells * me, own_cells), own_cells)
        up[d, me] = w_src[d, own]

        def chain_copy():
            to = lax.rem(x + (nx - 1 if flip else 1), nx)
            return copy(v_src.at[d], v_dst.at[d], chain_s.at[d], chain_r.at[d], (z, y, to, b))

        def chain(k):
            sender = nx - 1 - k if flip else k
            if k >= nx - 1:
                return

            @pl.when(x == sender)
            def _():
                if k == 0:
                    v_src[d] = c_buf[d]
                else:
                    chain_copy().wait_recv()
                    v_src[d] = coarse_of(v_dst[d], flip) + c_buf[d]
                chain_copy().start()

        extra_up()
        chain(0)
        pieces = up.at[d, 0 : plane - 1]
        if plane > 1:
            copy(pieces, pieces, up_s.at[d], up_r.at[d], partner).wait_recv()
        row_total = [sum(up[d, r * nx + i] for i in range(nx)) for r in range(ny)]
        tz[d, z] = sum(times(row_total[r], column_later[r], flip) for r in range(ny))
        for k in z_steps:
            to = lax.rem(z + k, nz)
            copy(tz.at[d, z], tz.at[d, z], z_s.at[d], z_r.at[d, k], (to, y, x, b)).start()
        if not flip:
            z_mats.pass_on(early)
        inside = [None] * ny
        order = list(range(ny - 1, -1, -1)) if flip else list(range(ny))
        inside[order[0]] = jnp.zeros((own_cells, ch), F32)
        for r, s in zip(order, order[1:]):
            inside[s] = times(inside[r], ry[r], flip) + row_total[r]
        chain(1)

        def total_from(k):
            source = lax.rem(z - k + nz, nz)
            return copy(tz.at[d, source], tz.at[d, source], z_s.at[d], z_r.at[d, k], partner)

        entering[...] = jnp.zeros((own_cells, ch), F32)
        for i in range(nz - 1, 0, -1) if flip else range(nz - 1):

            @pl.when(z < i if flip else z > i)
            def _():
                k = lax.rem(z - i + nz, nz)
                total_from(k).wait_recv()
                if i == (nz - 1 if flip else 0):
                    entering[...] = tz[d, i]
                else:
                    z_mats.swap(i, k, other).wait_recv()
                    entering[...] = times(entering[...], pz[i], flip) + tz[d, i]

        for r in range(ny):
            row_src[d, r] = times(entering[...], column_sooner[r], flip) + inside[r]
        for o in offsets:
            ty, _, to = mate(o)
            copy(row_src.at[d, ty], down.at[d, own], down_s.at[d], down_r.at[d], to).start()
        down[d, own] = row_src[d, y]
        for k in range(2, nx - 1):
            chain(k)
        if not flip:
            z_mats.pass_on(late, far=False)
        if plane > 1:
            copy(pieces, pieces, down_s.at[d], down_r.at[d], partner).wait_recv()
        results[d] = times(down[d], row_sooner[x], flip)

        if nx > 1:

            @pl.when(x == (0 if flip else nx - 1))
            def _():
                chain_copy().wait_recv()

            @pl.when(x != (nx - 1 if flip else 0))
            def _():
                results[d] = results[d] + v_dst[d]

        def drain():
            if plane > 1:
                copy(pieces, pieces, up_s.at[d], up_r.at[d], partner).wait_send()
                copy(pieces, pieces, down_s.at[d], down_r.at[d], partner).wait_send()
            totals = tz.at[d, 0 : nz - 1]
            copy(totals, totals, z_s.at[d], z_r.at[d, 0], partner).wait_send()
            for i in range(nz):

                @pl.when(z > i if flip else z < i)
                def _():
                    k = lax.rem(z - i + nz, nz)
                    total_from(k).wait_recv()

            if nx > 1:

                @pl.when(x != (0 if flip else nx - 1))
                def _():
                    chain_copy().wait_send()

        return drain

    pl.when(pos != 0)(forward_shift.wait_recv)
    start = jnp.where(first, states[...], shift_dst[0])
    c_buf[0] = jnp.where(first, 0.0, -coarse_of(start, False)) + relax(start)

    def extra_up():
        column_mats.pass_on()
        column_mats.finish()
        middle_y = (ny + 1) // 2
        pr[0] = eye
        sr[ny - 1] = eye

        def sooner(j):
            pr[j] = ry[0] if j == 1 else times(pr[j - 1], ry[j - 1])

        def later(j):
            sr[j] = ry[j + 1] if j == ny - 2 else times(ry[j + 1], sr[j + 1])

        for j in range(1, middle_y + 1):
            sooner(j)
        for j in range(ny - 2, middle_y - 2, -1):
            later(j)
        pz[z] = times(pr[middle_y], sr[middle_y - 1]) if ny > 1 else pr[1]
        z_mats.start()
        for j in range(middle_y + 1, ny):
            sooner(j)
        for j in range(middle_y - 2, -1, -1):
            later(j)

    forward_drain = scan(0, extra_up)
    results[0] = jnp.where(first, states[...], results[0])
    pltpu.make_async_copy(results.at[0], ns_out, out_sem.at[0]).start()

    def final_step(n, u):
        u_all[b, n] = u
        activ = activate(n, u)
        slopes[n] = 1.0 - activ * activ
        return u + STEP * activ

    lax.fori_loop(0, blocks, final_step, results[0], unroll=True)
    inputs_copy = copy(u_all.at[b], u_all.at[b], u_s, u_r, partner)
    inputs_copy.start()

    shift_src[1] = back_relax(guess[...])
    back_shift = copy(shift_src.at[1], shift_dst.at[1], shift_s.at[1], shift_r.at[1], behind)
    pl.when(pos != 0)(back_shift.start)
    new_ends = jnp.where(first, 0.0, coarse_of(results[0], False)) + c_buf[0]
    v_src[2] = new_ends
    pltpu.make_async_copy(v_src.at[2], ne_out, out_sem.at[0]).start()
    inputs_copy.wait_recv()
    for n in range(blocks):
        for i in range(nb):
            xt[n, :, cells * i : cells * (i + 1)] = beside(u_all[i, n])
    inputs_out = pltpu.make_async_copy(xt, xt_out, out_sem.at[1])
    inputs_out.start()
    z_mats.pass_on(late, near=False)
    pl.when(pos != last)(back_shift.wait_recv)
    back_start = jnp.where(final, guess[...], shift_dst[1])
    c_buf[1] = jnp.where(final, 0.0, -coarse_of(back_start, True)) + back_relax(back_start)
    back_drain = scan(1, lambda: None)
    results[1] = jnp.where(final, guess[...], results[1])
    pltpu.make_async_copy(results.at[1], na_out, out_sem.at[0]).start()

    def sens_copy(n):
        return copy(sens_all.at[n, b], sens_all.at[n, b], sens_s, sens_r.at[n], partner)

    lam_ref[...] = results[1]
    for n in range(blocks - 1, -1, -1):
        sens = slopes[n] * lam_ref[...]
        sens_all[n, b] = sens
        sens_copy(n).start()
        if n > 0:
            place(sens)
            lam_ref[...] = lam_ref[...] + STEP * adjoint_conv(n)
    new_back = jnp.where(final, 0.0, coarse_of(results[1], True)) + c_buf[1]
    v_src[3] = new_back
    pltpu.make_async_copy(v_src.at[3], nb_out, out_sem.at[0]).start()
    for n in range(blocks - 1, -1, -1):
        got = sens_all.at[n, 1 - b]
        copy(got, got, sens_s, sens_r.at[n], partner).wait_recv()
        pltpu.make_async_copy(sens_all.at[n], sens_out.at[n], out_sem.at[2]).start()

    copy(u_all.at[0], u_all.at[0], sens_s, u_r, partner).wait_send()
    inputs_copy.wait_send()
    pl.when(pos != last)(forward_shift.wait_send)
    pl.when(pos != 0)(back_shift.wait_send)
    row_mats.drain()
    column_mats.drain()
    z_mats.drain()
    for i in {0, nz - 1}:

        @pl.when(z != i)
        def _():
            z_mats.swap(i, lax.rem(z - i + nz, nz), other).wait_recv()

    forward_drain()
    back_drain()
    pltpu.make_async_copy(v_src, v_src, out_sem.at[0]).wait()
    inputs_out.wait()
    pltpu.make_async_copy(sens_all, sens_out, out_sem.at[2]).wait()


def gradients(
    factor, side,
    ns, ne, na, nb, xt, sens,
    ns_out, ne_out, na_out, nb_out, gk_out, gb_out,
    xs, grads, bias_grads, out_sem,
):
    blocks, images, cells, ch = sens.shape
    outs = [
        pltpu.make_async_copy(a, out, out_sem.at[blocks + 1 + i])
        for i, (a, out) in enumerate(((ns, ns_out), (ne, ne_out), (na, na_out), (nb, nb_out)))
    ]
    for c in outs:
        c.start()
    for i in range(images):
        xs[i, 0:side, :] = jnp.zeros((side, ch), BF16)
        xs[i, side + cells : 2 * side + cells, :] = jnp.zeros((side, ch), BF16)
    for n in range(blocks):
        bias_sum = jnp.zeros((1, ch), F32)
        for i in range(images):
            rounded = sens[n, i].astype(BF16)
            xs[i, side : side + cells, :] = rounded
            bias_sum = bias_sum + jnp.sum(rounded.astype(F32), axis=0, keepdims=True)
        bias_grads[n : n + 1, :] = factor * bias_sum
        rows = [
            jnp.concatenate([xs[i, side * dy : side * dy + cells, :] for dy in (2, 1, 0)], axis=1)
            for i in range(images)
        ]
        total = factor * dot(xt[n], jnp.concatenate(rows, axis=0))
        for dy in range(3):
            for dx in range(3):
                grads[n, 3 * dy + dx] = total[ch * dx : ch * (dx + 1), ch * dy : ch * (dy + 1)]
        outs.append(pltpu.make_async_copy(grads.at[n], gk_out.at[n], out_sem.at[n]))
        outs[-1].start()
    outs.append(pltpu.make_async_copy(bias_grads, gb_out, out_sem.at[blocks]))
    outs[-1].start()
    for c in outs:
        c.wait()


def body(sizes, kernels, biases, states, adjoint_guess):
    nz, ny, nx, nb = sizes
    plane = ny * nx
    blocks, taps, ch, _ = kernels.shape
    side = states.shape[2]
    batch = states.shape[1]
    cells = side * side
    own = cells // plane
    field = jax.ShapeDtypeStruct((cells, ch), F32)
    dma = pltpu.SemaphoreType.DMA
    vmem = pltpu.VMEM
    scratch = [
        vmem((blocks, taps * ch, ch), BF16),
        vmem((blocks, ch), F32),
        vmem((cells, ch), F32),
        vmem((cells, ch), F32),
        vmem((ch, ch), BF16),
        vmem((cells + 2 * side, ch), BF16),
        vmem((blocks, 3 * ch, nb * cells), BF16),
        vmem((blocks, cells, ch), F32),
        vmem((nx, ch, ch), F32),
        vmem((ny, ch, ch), F32),
        vmem((nz, ch, ch), F32),
        vmem((nx + 1, ch, ch), F32),
        vmem((nx, ch, ch), F32),
        vmem((ny + 1, ch, ch), F32),
        vmem((ny, ch, ch), F32),
        vmem((2, cells, ch), F32),
        vmem((2, cells, ch), F32),
        vmem((2, cells, ch), F32),
        vmem((4, cells, ch), F32),
        vmem((2, cells, ch), F32),
        vmem((2, cells, ch), F32),
        vmem((2, plane, own, ch), F32),
        vmem((2, nz, own, ch), F32),
        vmem((own, ch), F32),
        vmem((2, ny, own, ch), F32),
        vmem((2, cells, ch), F32),
        vmem((2, cells, ch), F32),
        vmem((cells, ch), F32),
        vmem((nb, blocks, cells, ch), F32),
        vmem((blocks, nb, cells, ch), F32),
        dma((4 + blocks,)),
        dma((3,)),
        dma((6,)),
        dma((nx,)),
        dma((nx,)),
        dma((ny,)),
        dma((ny,)),
        dma((nz,)),
        dma((nz,)),
        dma((2,)),
        dma((2,)),
        dma((2,)),
        dma((2,)),
        dma((2,)),
        dma((2,)),
        dma((2,)),
        dma((2, nz)),
        dma((2,)),
        dma((2,)),
        dma(()),
        dma(()),
        dma(()),
        dma((blocks,)),
    ]
    any_space = pl.BlockSpec(memory_space=pl.ANY)
    outs = pl.pallas_call(
        functools.partial(kernel, sizes, blocks, side),
        out_shape=[field] * 4
        + [
            jax.ShapeDtypeStruct((blocks, 3 * ch, nb * cells), BF16),
            jax.ShapeDtypeStruct((blocks, nb, cells, ch), F32),
        ],
        in_specs=[pl.BlockSpec(memory_space=pltpu.HBM)] * 4,
        out_specs=[any_space] * 6,
        scratch_shapes=scratch,
        compiler_params=pltpu.CompilerParams(
            collective_id=0, has_side_effects=True, vmem_limit_bytes=40 * 1024 * 1024
        ),
        name="vcycle",
    )(
        *(
            pltpu.with_memory_space_constraint(a, pltpu.HBM)
            for a in (
                kernels.reshape(blocks, taps * ch, ch),
                biases,
                states.reshape(cells, ch),
                adjoint_guess.reshape(cells, ch),
            )
        )
    )
    outs = pl.pallas_call(
        functools.partial(gradients, STEP / (nb * batch * cells), side),
        out_shape=[field] * 4
        + [jax.ShapeDtypeStruct((blocks, taps, ch, ch), F32), jax.ShapeDtypeStruct((blocks, ch), F32)],
        in_specs=[any_space] * 4 + [pl.BlockSpec(memory_space=vmem)] * 2,
        out_specs=[pl.BlockSpec(memory_space=pltpu.HBM)] * 6,
        scratch_shapes=[
            vmem((nb, cells + 2 * side, ch), BF16),
            vmem((blocks, taps, ch, ch), F32),
            vmem((blocks, ch), F32),
            dma((blocks + 5,)),
        ],
        compiler_params=pltpu.CompilerParams(vmem_limit_bytes=16 * 1024 * 1024),
        name="gradients",
    )(*outs)
    fields = [out.reshape(states.shape) for out in outs[:4]]
    return (*fields, outs[4], outs[5])


def solution(mesh, sizes=(8, 4, 4)):
    sizes = (*sizes, mesh.shape["batch"])
    torus = Mesh(mesh.devices.reshape(sizes), AXES)
    state = P(LAYER, "batch", None, None, None)
    return jax.shard_map(
        functools.partial(body, sizes),
        mesh=torus,
        in_specs=(P(LAYER, None, None, None), P(LAYER, None), state, state),
        out_specs=(state, state, state, state, P(LAYER, None, None, None), P(LAYER, None)),
        check_vma=False,
    )
```

```python
import functools

import jax
import jax.numpy as jnp
from jax import lax
from jax.experimental import pallas as pl
from jax.experimental.pallas import tpu as pltpu
from jax.sharding import Mesh
from jax.sharding import PartitionSpec as P

LAYER = ("layer_0", "layer_1", "layer_2")
AXES = LAYER + ("batch",)
MESH = pl.DeviceIdType.MESH
STEP = 0.1
F32 = jnp.float32
BF16 = jnp.bfloat16


def split(value):
    high = value.astype(BF16)
    return high, (value - high.astype(F32)).astype(BF16)


def dot(left, right, flip=False):
    contract = (((1,), (1,)), ((), ())) if flip else (((1,), (0,)), ((), ()))
    return lax.dot_general(left, right, contract, preferred_element_type=F32)


def times_exact(left, exact, flip=False):
    high, low = split(left)
    return dot(high, exact, flip) + dot(low, exact, flip)


def exact_times(exact, right):
    high, low = split(right)
    return dot(exact, high) + dot(exact, low)


def times(left, right, flip=False):
    high, low = split(left)
    right_high, right_low = split(right)
    return dot(high, right_high, flip) + (dot(low, right_high, flip) + dot(high, right_low, flip))


def kernel(
    sizes, blocks, side,
    k_hbm, b_hbm, st_hbm, ad_hbm,
    ns_out, ne_out, na_out, nb_out, xt_out, sens_out,
    w, bias, states, guess, middle,
    xs, xt, slopes,
    kx, ry, pz, pm, sm, pr, sr,
    shift_src, shift_dst, c_buf, v_src, v_dst,
    w_src, up, tz, entering, row_src, down, results, lam_ref,
    u_all, sens_all,
    in_sem, out_sem,
    mat_s, x_r, xp_r, y_r, yp_r, zm_r, zp_r,
    shift_s, shift_r, chain_s, chain_r,
    up_s, up_r, z_s, z_r, down_s, down_r,
    u_s, u_r, sens_s, sens_r,
):
    nz, ny, nx, nb = sizes
    plane = ny * nx
    ch = w.shape[-1]
    cells = side * side
    own_cells = cells // plane
    coarse_step = blocks * STEP
    z, y, x = (lax.axis_index(a) for a in LAYER)
    b = lax.axis_index("batch")
    me = y * nx + x
    pos = z * plane + me
    last = nz * plane - 1
    first = pos == 0
    final = pos == last

    def device(position):
        return (position // plane, lax.rem(position // nx, ny), lax.rem(position, nx), b)

    ahead = device(lax.rem(pos + 1, last + 1))
    behind = device(lax.rem(pos + last, last + 1))
    partner = (z, y, x, 1 - b)

    def ring(step, size):
        return min(step, size - step)

    offsets = sorted(
        ((dy, dx) for dy in range(ny) for dx in range(nx) if dy or dx),
        key=lambda o: -ring(o[0], ny) - ring(o[1], nx),
    )
    z_steps = sorted(range(1, nz), key=lambda k: -ring(k, nz))

    def mate(offset):
        ty, tx = lax.rem(y + offset[0], ny), lax.rem(x + offset[1], nx)
        return ty, ty * nx + tx, (z, ty, tx, b)

    def copy(src, dst, send, recv, to):
        return pltpu.make_async_remote_copy(
            src_ref=src, dst_ref=dst, send_sem=send, recv_sem=recv, device_id=to, device_id_type=MESH
        )

    weight_loads = [pltpu.make_async_copy(k_hbm.at[n], w.at[n], in_sem.at[4 + n]) for n in range(blocks)]
    first_loads = [
        pltpu.make_async_copy(st_hbm, states, in_sem.at[0]),
        pltpu.make_async_copy(b_hbm, bias, in_sem.at[1]),
    ]
    later_loads = [
        pltpu.make_async_copy(k_hbm.at[0, 4 * ch : 5 * ch], middle, in_sem.at[2]),
        pltpu.make_async_copy(ad_hbm, guess, in_sem.at[3]),
    ]
    for c in (weight_loads[0], *first_loads, *weight_loads[1:], *later_loads):
        c.start()

    barrier = pltpu.get_barrier_semaphore()

    def greet(to):
        pl.semaphore_signal(barrier, inc=1, device_id=to, device_id_type=MESH)

    greet(ahead)
    greet(behind)
    greet(partner)
    for o in offsets:
        greet(mate(o)[2])
    for k in range(1, nz):
        greet((lax.rem(z + k, nz), y, x, b))
    greeted = 3 + plane - 1 + nz - 1

    xs[0:side, :] = jnp.zeros((side, ch), BF16)
    xs[side + cells : 2 * side + cells, :] = jnp.zeros((side, ch), BF16)

    @pl.when(first)
    def _():
        shift_dst[0] = jnp.zeros((cells, ch), F32)

    @pl.when(final)
    def _():
        shift_dst[1] = jnp.zeros((cells, ch), F32)

    column = lax.rem(lax.broadcasted_iota(jnp.int32, (cells, ch), 0), side)
    inner_left = column != 0
    inner_right = column != side - 1

    def place(value):
        xs[side : side + cells, :] = value.astype(BF16)

    def rows_beside():
        return [xs[side * dy : side * dy + cells, :] for dy in range(3)]

    def from_left(value):
        return jnp.where(inner_left, pltpu.roll(value, 1, 0), 0.0)

    def from_right(value):
        return jnp.where(inner_right, pltpu.roll(value, cells - 1, 0), 0.0)

    def join_columns(wide):
        return wide[:, ch : 2 * ch] + (from_left(wide[:, :ch]) + from_right(wide[:, 2 * ch :]))

    def tap(n, t):
        return w[n, ch * t : ch * (t + 1), :]

    def activate(n, u):
        place(u)
        weights = jnp.concatenate(
            [jnp.concatenate([tap(n, 3 * dy + dx) for dx in range(3)], axis=1) for dy in range(3)], axis=0
        )
        wide = dot(jnp.concatenate(rows_beside(), axis=1), weights)
        return jnp.tanh(join_columns(wide) + bias[pl.ds(n, 1), :])

    def adjoint_conv(n):
        flipped = jnp.concatenate(
            [jnp.concatenate([tap(n, 8 - 3 * dy - dx) for dy in range(3)], axis=1) for dx in range(3)], axis=0
        )
        return join_columns(dot(jnp.concatenate(rows_beside(), axis=1), flipped, True))

    def beside(u):
        return jnp.concatenate([jnp.transpose(v).astype(BF16) for v in (from_left(u), u, from_right(u))], axis=0)

    def relax(u):
        return lax.fori_loop(0, blocks, lambda n, s: s + STEP * activate(n, s), u, unroll=True)

    def back_relax(lam):
        def body(k, lam):
            n = blocks - 1 - k
            place(slopes[n] * lam)
            return lam + STEP * adjoint_conv(n)

        return lax.fori_loop(0, blocks, body, lam, unroll=True)

    eye = (
        lax.broadcasted_iota(jnp.int32, (ch, ch), 0) == lax.broadcasted_iota(jnp.int32, (ch, ch), 1)
    ).astype(F32)
    half = ch // nb
    mine = pl.ds(pl.multiple_of(half * b, half), half)
    other = pl.ds(pl.multiple_of(half * (1 - b), half), half)

    class Maps:
        def __init__(self, buf, index, size, to, send, recv, pair_send, pair_recv):
            self.buf, self.index, self.size, self.to = buf, index, size, to
            self.send, self.recv, self.pair_send, self.pair_recv = send, recv, pair_send, pair_recv
            near = [k for k in range(1, size) if ring(k, size) <= 2]
            near.sort(key=lambda k: -ring(k, size))
            far = [k for k in range(size - 1, 0, -1) if ring(k, size) > 2]
            self.near, self.far = near, far

        def source(self, k):
            return lax.rem(self.index - k + self.size, self.size)

        def move(self, source, k, target):
            part = self.buf.at[source, mine]
            return copy(part, part, self.send, self.recv.at[k], target)

        def swap(self, source, k, rows):
            part = self.buf.at[source, rows]
            return copy(part, part, self.pair_send, self.pair_recv.at[k], partner)

        def start(self):
            for k in self.near:
                self.move(self.index, k, self.to(lax.rem(self.index + k, self.size))).start()

        def pass_on(self, wanted=None, near=True, far=True):
            order = self.near if self.far else self.near[::-1]
            for k in (order if near else []) + (self.far if far else []):
                source = self.source(k)

                def take(k=k, source=source):
                    self.move(source, k, partner).wait_recv()
                    for f in self.far:
                        if k == (2 if f <= self.size // 2 else self.size - 2):
                            self.move(source, f, self.to(lax.rem(self.index + f - k + self.size, self.size))).start()
                    self.swap(source, k, mine).start()

                if wanted is None:
                    take()
                else:
                    pl.when(wanted(k, source))(take)

        def finish(self):
            for k in range(1, self.size):
                self.swap(self.source(k), k, other).wait_recv()

        def drain(self):
            if self.size > 1:
                part = self.buf.at[0 : self.size - 1, mine]
                copy(part, part, self.send, self.recv.at[0], partner).wait_send()
                copy(part, part, self.pair_send, self.recv.at[0], partner).wait_send()

    row_mats = Maps(kx, x, nx, lambda t: (z, y, t, b), mat_s.at[0], x_r, mat_s.at[1], xp_r)
    column_mats = Maps(ry, y, ny, lambda t: (z, t, x, b), mat_s.at[2], y_r, mat_s.at[3], yp_r)
    z_mats = Maps(pz, z, nz, lambda t: (t, y, x, b), mat_s.at[4], zm_r, mat_s.at[5], zp_r)

    for c in first_loads:
        c.wait()
    relaxed = states[...]
    for n in range(blocks):
        weight_loads[n].wait()
        relaxed = relaxed + STEP * activate(n, relaxed)
    for c in later_loads:
        c.wait()
    kx[x] = middle[...].astype(F32)
    pl.semaphore_wait(barrier, greeted)
    row_mats.start()
    shift_src[0] = relaxed
    forward_shift = copy(shift_src.at[0], shift_dst.at[0], shift_s.at[0], shift_r.at[0], ahead)
    pl.when(pos != last)(forward_shift.start)

    row_mats.pass_on()
    row_mats.finish()
    def step_map(j):
        return eye + coarse_step * kx[j]

    middle_x = (nx + 1) // 2
    pm[0] = eye
    sm[nx - 1] = eye

    def row_sooner_map(j):
        pm[j] = step_map(0) if j == 1 else pm[j - 1] + coarse_step * times_exact(pm[j - 1], kx[j - 1].astype(BF16))

    def row_later_map(j):
        first_later = step_map(j + 1)
        sm[j] = first_later if j == nx - 2 else sm[j + 1] + coarse_step * exact_times(kx[j + 1].astype(BF16), sm[j + 1])

    for j in range(1, middle_x + 1):
        row_sooner_map(j)
    for j in range(nx - 2, middle_x - 2, -1):
        row_later_map(j)
    ry[y] = times(pm[middle_x], sm[middle_x - 1]) if nx > 1 else pm[1]
    column_mats.start()
    for j in range(middle_x + 1, nx):
        row_sooner_map(j)
    for j in range(middle_x - 2, -1, -1):
        row_later_map(j)

    def early(k, source):
        needed = (source < z) & (source != 0)
        return needed | (z == 0) if k == nz - 2 and nz > 4 else needed

    def late(k, source):
        return jnp.logical_not(early(k, source))

    def coarse_of(field, flip):
        return field + coarse_step * times_exact(field, middle[...], flip)

    def scan(d, extra_up):
        flip = d == 1
        row_later, row_sooner = (pm, sm) if flip else (sm, pm)
        column_later, column_sooner = (pr, sr) if flip else (sr, pr)
        w_src[d] = times(c_buf[d], row_later[x], flip)
        for o in offsets:
            _, t, to = mate(o)
            piece = pl.ds(pl.multiple_of(own_cells * t, own_cells), own_cells)
            copy(w_src.at[d, piece], up.at[d, me], up_s.at[d], up_r.at[d], to).start()
        own = pl.ds(pl.multiple_of(own_cells * me, own_cells), own_cells)
        up[d, me] = w_src[d, own]

        def chain_copy():
            to = lax.rem(x + (nx - 1 if flip else 1), nx)
            return copy(v_src.at[d], v_dst.at[d], chain_s.at[d], chain_r.at[d], (z, y, to, b))

        def chain(k):
            sender = nx - 1 - k if flip else k
            if k >= nx - 1:
                return

            @pl.when(x == sender)
            def _():
                if k == 0:
                    v_src[d] = c_buf[d]
                else:
                    chain_copy().wait_recv()
                    v_src[d] = coarse_of(v_dst[d], flip) + c_buf[d]
                chain_copy().start()

        extra_up()
        chain(0)
        pieces = up.at[d, 0 : plane - 1]
        if plane > 1:
            copy(pieces, pieces, up_s.at[d], up_r.at[d], partner).wait_recv()
        row_total = [sum(up[d, r * nx + i] for i in range(nx)) for r in range(ny)]
        tz[d, z] = sum(times(row_total[r], column_later[r], flip) for r in range(ny))
        for k in z_steps:
            to = lax.rem(z + k, nz)
            copy(tz.at[d, z], tz.at[d, z], z_s.at[d], z_r.at[d, k], (to, y, x, b)).start()
        if not flip:
            z_mats.pass_on(early)
        inside = [None] * ny
        order = list(range(ny - 1, -1, -1)) if flip else list(range(ny))
        inside[order[0]] = jnp.zeros((own_cells, ch), F32)
        for r, s in zip(order, order[1:]):
            inside[s] = times(inside[r], ry[r], flip) + row_total[r]
        chain(1)

        def total_from(k):
            source = lax.rem(z - k + nz, nz)
            return copy(tz.at[d, source], tz.at[d, source], z_s.at[d], z_r.at[d, k], partner)

        entering[...] = jnp.zeros((own_cells, ch), F32)
        for i in range(nz - 1, 0, -1) if flip else range(nz - 1):

            @pl.when(z < i if flip else z > i)
            def _():
                k = lax.rem(z - i + nz, nz)
                total_from(k).wait_recv()
                if i == (nz - 1 if flip else 0):
                    entering[...] = tz[d, i]
                else:
                    z_mats.swap(i, k, other).wait_recv()
                    entering[...] = times(entering[...], pz[i], flip) + tz[d, i]

        for r in range(ny):
            row_src[d, r] = times(entering[...], column_sooner[r], flip) + inside[r]
        for o in offsets:
            ty, _, to = mate(o)
            copy(row_src.at[d, ty], down.at[d, own], down_s.at[d], down_r.at[d], to).start()
        down[d, own] = row_src[d, y]
        for k in range(2, nx - 1):
            chain(k)
        if not flip:
            z_mats.pass_on(late, far=False)
        if plane > 1:
            copy(pieces, pieces, down_s.at[d], down_r.at[d], partner).wait_recv()
        results[d] = times(down[d], row_sooner[x], flip)

        if nx > 1:

            @pl.when(x == (0 if flip else nx - 1))
            def _():
                chain_copy().wait_recv()

            @pl.when(x != (nx - 1 if flip else 0))
            def _():
                results[d] = results[d] + v_dst[d]

        def drain():
            if plane > 1:
                copy(pieces, pieces, up_s.at[d], up_r.at[d], partner).wait_send()
                copy(pieces, pieces, down_s.at[d], down_r.at[d], partner).wait_send()
            totals = tz.at[d, 0 : nz - 1]
            copy(totals, totals, z_s.at[d], z_r.at[d, 0], partner).wait_send()
            for i in range(nz):

                @pl.when(z > i if flip else z < i)
                def _():
                    k = lax.rem(z - i + nz, nz)
                    total_from(k).wait_recv()

            if nx > 1:

                @pl.when(x != (0 if flip else nx - 1))
                def _():
                    chain_copy().wait_send()

        return drain

    pl.when(pos != 0)(forward_shift.wait_recv)
    start = jnp.where(first, states[...], shift_dst[0])
    c_buf[0] = jnp.where(first, 0.0, -coarse_of(start, False)) + relax(start)

    def extra_up():
        column_mats.pass_on()
        column_mats.finish()
        middle_y = (ny + 1) // 2
        pr[0] = eye
        sr[ny - 1] = eye

        def sooner(j):
            pr[j] = ry[0] if j == 1 else times(pr[j - 1], ry[j - 1])

        def later(j):
            sr[j] = ry[j + 1] if j == ny - 2 else times(ry[j + 1], sr[j + 1])

        for j in range(1, middle_y + 1):
            sooner(j)
        for j in range(ny - 2, middle_y - 2, -1):
            later(j)
        pz[z] = times(pr[middle_y], sr[middle_y - 1]) if ny > 1 else pr[1]
        z_mats.start()
        for j in range(middle_y + 1, ny):
            sooner(j)
        for j in range(middle_y - 2, -1, -1):
            later(j)

    forward_drain = scan(0, extra_up)
    results[0] = jnp.where(first, states[...], results[0])
    pltpu.make_async_copy(results.at[0], ns_out, out_sem.at[0]).start()

    def final_step(n, u):
        u_all[b, n] = u
        activ = activate(n, u)
        slopes[n] = 1.0 - activ * activ
        return u + STEP * activ

    lax.fori_loop(0, blocks, final_step, results[0], unroll=True)
    inputs_copy = copy(u_all.at[b], u_all.at[b], u_s, u_r, partner)
    inputs_copy.start()

    shift_src[1] = back_relax(guess[...])
    back_shift = copy(shift_src.at[1], shift_dst.at[1], shift_s.at[1], shift_r.at[1], behind)
    pl.when(pos != 0)(back_shift.start)
    new_ends = jnp.where(first, 0.0, coarse_of(results[0], False)) + c_buf[0]
    v_src[2] = new_ends
    pltpu.make_async_copy(v_src.at[2], ne_out, out_sem.at[0]).start()
    inputs_copy.wait_recv()
    for n in range(blocks):
        for i in range(nb):
            xt[n, :, cells * i : cells * (i + 1)] = beside(u_all[i, n])
    inputs_out = pltpu.make_async_copy(xt, xt_out, out_sem.at[1])
    inputs_out.start()
    z_mats.pass_on(late, near=False)
    pl.when(pos != last)(back_shift.wait_recv)
    back_start = jnp.where(final, guess[...], shift_dst[1])
    c_buf[1] = jnp.where(final, 0.0, -coarse_of(back_start, True)) + back_relax(back_start)
    back_drain = scan(1, lambda: None)
    results[1] = jnp.where(final, guess[...], results[1])
    pltpu.make_async_copy(results.at[1], na_out, out_sem.at[0]).start()

    def sens_copy(n):
        return copy(sens_all.at[n, b], sens_all.at[n, b], sens_s, sens_r.at[n], partner)

    lam_ref[...] = results[1]
    for n in range(blocks - 1, -1, -1):
        sens = slopes[n] * lam_ref[...]
        sens_all[n, b] = sens
        sens_copy(n).start()
        if n > 0:
            place(sens)
            lam_ref[...] = lam_ref[...] + STEP * adjoint_conv(n)
    new_back = jnp.where(final, 0.0, coarse_of(results[1], True)) + c_buf[1]
    v_src[3] = new_back
    pltpu.make_async_copy(v_src.at[3], nb_out, out_sem.at[0]).start()
    for n in range(blocks - 1, -1, -1):
        got = sens_all.at[n, 1 - b]
        copy(got, got, sens_s, sens_r.at[n], partner).wait_recv()
        pltpu.make_async_copy(sens_all.at[n], sens_out.at[n], out_sem.at[2]).start()

    copy(u_all.at[0], u_all.at[0], sens_s, u_r, partner).wait_send()
    inputs_copy.wait_send()
    pl.when(pos != last)(forward_shift.wait_send)
    pl.when(pos != 0)(back_shift.wait_send)
    row_mats.drain()
    column_mats.drain()
    z_mats.drain()
    for i in {0, nz - 1}:

        @pl.when(z != i)
        def _():
            z_mats.swap(i, lax.rem(z - i + nz, nz), other).wait_recv()

    forward_drain()
    back_drain()
    pltpu.make_async_copy(v_src, v_src, out_sem.at[0]).wait()
    inputs_out.wait()
    pltpu.make_async_copy(sens_all, sens_out, out_sem.at[2]).wait()


def gradients(
    factor, side,
    ns, ne, na, nb, xt, sens,
    ns_out, ne_out, na_out, nb_out, gk_out, gb_out,
    xs, grads, bias_grads, out_sem,
):
    blocks, images, cells, ch = sens.shape
    outs = [
        pltpu.make_async_copy(a, out, out_sem.at[blocks + 1 + i])
        for i, (a, out) in enumerate(((ns, ns_out), (ne, ne_out), (na, na_out), (nb, nb_out)))
    ]
    for c in outs:
        c.start()
    for i in range(images):
        xs[i, 0:side, :] = jnp.zeros((side, ch), BF16)
        xs[i, side + cells : 2 * side + cells, :] = jnp.zeros((side, ch), BF16)
    for n in range(blocks):
        bias_sum = jnp.zeros((1, ch), F32)
        for i in range(images):
            rounded = sens[n, i].astype(BF16)
            xs[i, side : side + cells, :] = rounded
            bias_sum = bias_sum + jnp.sum(rounded.astype(F32), axis=0, keepdims=True)
        bias_grads[n : n + 1, :] = factor * bias_sum
        rows = [
            jnp.concatenate([xs[i, side * dy : side * dy + cells, :] for dy in (2, 1, 0)], axis=1)
            for i in range(images)
        ]
        total = factor * dot(xt[n], jnp.concatenate(rows, axis=0))
        for dy in range(3):
            for dx in range(3):
                grads[n, 3 * dy + dx] = total[ch * dx : ch * (dx + 1), ch * dy : ch * (dy + 1)]
        outs.append(pltpu.make_async_copy(grads.at[n], gk_out.at[n], out_sem.at[n]))
        outs[-1].start()
    outs.append(pltpu.make_async_copy(bias_grads, gb_out, out_sem.at[blocks]))
    outs[-1].start()
    for c in outs:
        c.wait()


def body(sizes, kernels, biases, states, adjoint_guess):
    nz, ny, nx, nb = sizes
    plane = ny * nx
    blocks, taps, ch, _ = kernels.shape
    side = states.shape[2]
    batch = states.shape[1]
    cells = side * side
    own = cells // plane
    field = jax.ShapeDtypeStruct((cells, ch), F32)
    dma = pltpu.SemaphoreType.DMA
    vmem = pltpu.VMEM
    scratch = [
        vmem((blocks, taps * ch, ch), BF16),
        vmem((blocks, ch), F32),
        vmem((cells, ch), F32),
        vmem((cells, ch), F32),
        vmem((ch, ch), BF16),
        vmem((cells + 2 * side, ch), BF16),
        vmem((blocks, 3 * ch, nb * cells), BF16),
        vmem((blocks, cells, ch), F32),
        vmem((nx, ch, ch), F32),
        vmem((ny, ch, ch), F32),
        vmem((nz, ch, ch), F32),
        vmem((nx + 1, ch, ch), F32),
        vmem((nx, ch, ch), F32),
        vmem((ny + 1, ch, ch), F32),
        vmem((ny, ch, ch), F32),
        vmem((2, cells, ch), F32),
        vmem((2, cells, ch), F32),
        vmem((2, cells, ch), F32),
        vmem((4, cells, ch), F32),
        vmem((2, cells, ch), F32),
        vmem((2, cells, ch), F32),
        vmem((2, plane, own, ch), F32),
        vmem((2, nz, own, ch), F32),
        vmem((own, ch), F32),
        vmem((2, ny, own, ch), F32),
        vmem((2, cells, ch), F32),
        vmem((2, cells, ch), F32),
        vmem((cells, ch), F32),
        vmem((nb, blocks, cells, ch), F32),
        vmem((blocks, nb, cells, ch), F32),
        dma((4 + blocks,)),
        dma((3,)),
        dma((6,)),
        dma((nx,)),
        dma((nx,)),
        dma((ny,)),
        dma((ny,)),
        dma((nz,)),
        dma((nz,)),
        dma((2,)),
        dma((2,)),
        dma((2,)),
        dma((2,)),
        dma((2,)),
        dma((2,)),
        dma((2,)),
        dma((2, nz)),
        dma((2,)),
        dma((2,)),
        dma(()),
        dma(()),
        dma(()),
        dma((blocks,)),
    ]
    any_space = pl.BlockSpec(memory_space=pl.ANY)
    outs = pl.pallas_call(
        functools.partial(kernel, sizes, blocks, side),
        out_shape=[field] * 4
        + [
            jax.ShapeDtypeStruct((blocks, 3 * ch, nb * cells), BF16),
            jax.ShapeDtypeStruct((blocks, nb, cells, ch), F32),
        ],
        in_specs=[pl.BlockSpec(memory_space=pltpu.HBM)] * 4,
        out_specs=[any_space] * 6,
        scratch_shapes=scratch,
        compiler_params=pltpu.CompilerParams(
            collective_id=0, has_side_effects=True, vmem_limit_bytes=40 * 1024 * 1024
        ),
        name="vcycle",
    )(
        *(
            pltpu.with_memory_space_constraint(a, pltpu.HBM)
            for a in (
                kernels.reshape(blocks, taps * ch, ch),
                biases,
                states.reshape(cells, ch),
                adjoint_guess.reshape(cells, ch),
            )
        )
    )
    outs = pl.pallas_call(
        functools.partial(gradients, STEP / (nb * batch * cells), side),
        out_shape=[field] * 4
        + [jax.ShapeDtypeStruct((blocks, taps, ch, ch), F32), jax.ShapeDtypeStruct((blocks, ch), F32)],
        in_specs=[any_space] * 4 + [pl.BlockSpec(memory_space=vmem)] * 2,
        out_specs=[pl.BlockSpec(memory_space=pltpu.HBM)] * 6,
        scratch_shapes=[
            vmem((nb, cells + 2 * side, ch), BF16),
            vmem((blocks, taps, ch, ch), F32),
            vmem((blocks, ch), F32),
            dma((blocks + 5,)),
        ],
        compiler_params=pltpu.CompilerParams(vmem_limit_bytes=16 * 1024 * 1024),
        name="gradients",
    )(*outs)
    fields = [out.reshape(states.shape) for out in outs[:4]]
    return (*fields, outs[4], outs[5])


def solution(mesh, sizes=(8, 4, 4)):
    sizes = (*sizes, mesh.shape["batch"])
    torus = Mesh(mesh.devices.reshape(sizes), AXES)
    state = P(LAYER, "batch", None, None, None)
    return jax.shard_map(
        functools.partial(body, sizes),
        mesh=torus,
        in_specs=(P(LAYER, None, None, None), P(LAYER, None), state, state),
        out_specs=(state, state, state, state, P(LAYER, None, None, None), P(LAYER, None)),
        check_vma=False,
    )
```
